512 devices in a mesh: tm: 32 (over z, core), rows: 8 (over x, y_lo), cols: 2 (over y_hi).
Axes of the slice: x: 4, y: 4 (y_hi: 2, y_lo: 2; y = y_hi * 2 + y_lo), z: 16, core: 2. Of those that a mesh axis runs over, the one named last changes fastest.
Arguments:
- iterate: float32 [1024, 8, 4, 128], P('tm', 'rows', 'cols'), may hold values from -6 to 6
- source: float32 [1024, 8, 4, 128], P('tm', 'rows', 'cols'), may hold values from -120 to 120
- initial: float32 [8, 4, 128], P('rows', 'cols'), may hold values from -6 to 6
- tile_basis: float32 [8, 4, 128, 128], P('rows', 'cols'), may hold values from -1 to 1, as said below
- tile_values: float32 [8, 4, 128], P('rows', 'cols'), may hold values from 16 to 48
- capacity: float32 [8, 4], P('rows', 'cols'), may hold values from 1 to 20
- tile_links: int32 [4, 8, 4, 128], P(None, 'rows', 'cols'), may hold values from 0 to 127
- conductance: float32 [4, 8, 4, 128], P(None, 'rows', 'cols'), may hold values from 0.5 to 3
Outputs:
- updated: float32 [1024, 8, 4, 128], P('tm', 'rows', 'cols')
The draws below stay inside these ranges and needn't reach their ends.
Inputs may be any that keep to these rules, and one draw needn't show every extreme that they name: `tile_basis`: each tile's basis has orthonormal columns.
All inputs are finite; a program needn't handle non-finite values.
Results may differ from the reference program's by a relative error of at most 0.0003.
Values sent between devices are 32-bit elements; how exact they have to be, the bound alone decides.
No kernel may reach another device: no remote copies, remote signals or barrier semaphores. Data moves between devices by JAX's collectives and lax.ppermute only.
A program may use at most 64 MiB of HBM per device.

```python
import math
import jax
import jax.numpy as jnp
from jax import lax

TILE = 128
STEPS = 1024
NTR = 8
NTC = 4


def draw_tile_basis(key, part):
    perm_key, sign_key = jax.random.split(key)
    count = NTR * NTC
    keys = jax.random.split(perm_key, count)
    order = jax.vmap(lambda one: jax.random.permutation(one, TILE))(keys).reshape(NTR, NTC, TILE, 1)
    signs = jax.random.randint(sign_key, (NTR, NTC, TILE, 1), 0, 2) * 2 - 1
    column = lax.broadcasted_iota(jnp.int32, (1, 1, 1, TILE), 3)
    phase = (2 * order + 1).astype(jnp.float32) * column.astype(jnp.float32) * (math.pi / (2.0 * TILE))
    norm = jnp.where(column == 0, math.sqrt(1.0 / TILE), math.sqrt(2.0 / TILE))
    return (signs.astype(jnp.float32) * norm * jnp.cos(phase)).astype(jnp.float32)


def with_ends(entries, key, low, high):
    extent = entries.shape
    spot = [jax.random.randint(jax.random.fold_in(key, axis), (), 0, extent[axis]) for axis in range(len(extent))]
    entries = entries.at[tuple(spot)].set(low)
    longest = extent.index(max(extent))
    spot[longest] = (spot[longest] + 1) % extent[longest]
    return entries.at[tuple(spot)].set(high)


def levels(own_key, shape, cuts, low, high):
    def one(axis_at, blocks):
        draws = jax.random.uniform(jax.random.fold_in(jax.random.fold_in(own_key, 6), axis_at), (blocks,), jnp.float32, low / len(cuts), high / len(cuts))
        return jnp.repeat(jnp.exp(draws), shape[axis_at] // blocks).reshape((-1,) + (1,) * (len(shape) - axis_at - 1))

    factor_of = one(*cuts[0])
    for cut in cuts[1:]:
        factor_of = factor_of * one(*cut)
    return factor_of


def centred(stream_key, dims, deviation, most, cuts=(), kind=jnp.bfloat16):
    values = jax.random.normal(stream_key, dims, jnp.float32) * deviation
    if len(cuts) > 0:
        values = levels(stream_key, dims, cuts, -0.22, 0.18) * values
    return jnp.clip(values, min=-most, max=most).astype(kind)


def setup_inputs(seed: int = 0) -> dict:
    splits = jax.random.split(jax.random.key(seed), 9)
    iterate = centred(splits[0], (STEPS, NTR, NTC, TILE), 1.0, 6.0, ((0, 32), (1, 8), (2, 2)), jnp.float32)
    source = centred(splits[1], (STEPS, NTR, NTC, TILE), 20.0, 120.0, ((0, 32), (1, 8), (2, 2)), jnp.float32)
    initial = centred(splits[2], (NTR, NTC, TILE), 1.0, 6.0, ((0, 8), (1, 2)), jnp.float32)
    tile_basis = draw_tile_basis(jax.random.fold_in(splits[8], 71), 0)
    tile_values = jnp.clip(jnp.exp(math.log(48.0) - 1.0986123 * jax.random.uniform(splits[4], (NTR, NTC, TILE), jnp.float32) ** levels(splits[4], (NTR, NTC, TILE), ((0, 8), (1, 2)), -0.2, 0.2)), 16.0, 48.0)
    capacity = jnp.clip(jnp.exp(math.log(20.0) - 2.9957323 * jax.random.uniform(splits[5], (NTR, NTC), jnp.float32) ** levels(splits[5], (NTR, NTC), ((0, 8), (1, 2)), -0.2, 0.2)), 1.0, 20.0)
    tile_links = with_ends(jax.random.randint(splits[6], (4, NTR, NTC, TILE), 0, TILE), jax.random.fold_in(splits[6], 1), 0, TILE - 1).astype(jnp.int32)
    conductance = jnp.clip(jnp.exp(math.log(3.0) - 1.7917595 * jax.random.uniform(splits[7], (4, NTR, NTC, TILE), jnp.float32) ** levels(splits[7], (4, NTR, NTC, TILE), ((1, 8), (2, 2)), -0.2, 0.2)), 0.5, 3.0)
    return {"iterate": iterate, "source": source, "initial": initial, "tile_basis": tile_basis, "tile_values": tile_values, "capacity": capacity, "tile_links": tile_links, "conductance": conductance}


circulant_alpha = 0.05
highest = lax.Precision.HIGHEST


def couple(field, tile_links, conductance):
    padded = jnp.pad(field, ((0, 0), (1, 1), (1, 1), (0, 0)))
    beside = (padded[:, :-2, 1:-1], padded[:, 2:, 1:-1], padded[:, 1:-1, :-2], padded[:, 1:-1, 2:])
    total = jnp.zeros_like(field)
    for direction in range(4):
        index_block = jnp.broadcast_to(tile_links[direction][None], field.shape).astype(jnp.int32)
        picked = jnp.take_along_axis(beside[direction], index_block, axis=3)
        total = total - conductance[direction][None] * picked
    return total


def apply_block(basis, values, field):
    proj = jnp.einsum("rcji,trcj->trci", basis, field, precision=highest)
    return jnp.einsum("rcij,trcj->trci", basis, values[None] * proj, precision=highest)


def spectral_solve(part_real, part_imag, basis, values, shift_real, shift_imag):
    proj_real = jnp.einsum("rcji,trcj->trci", basis, part_real, precision=highest)
    proj_imag = jnp.einsum("rcji,trcj->trci", basis, part_imag, precision=highest)
    den_real = values[None] + shift_real[..., None]
    den_imag = jnp.broadcast_to(shift_imag[..., None], den_real.shape)
    magnitude = den_real * den_real + den_imag * den_imag
    quot_real = (proj_real * den_real + proj_imag * den_imag) / magnitude
    quot_imag = (proj_imag * den_real - proj_real * den_imag) / magnitude
    out_real = jnp.einsum("rcij,trcj->trci", basis, quot_real, precision=highest)
    out_imag = jnp.einsum("rcij,trcj->trci", basis, quot_imag, precision=highest)
    return out_real, out_imag


def reference(iterate, source, initial, tile_basis, tile_values, capacity, tile_links, conductance):
    previous = jnp.concatenate([initial[None], iterate[:-1]], axis=0)
    within = apply_block(tile_basis, tile_values, iterate)
    residual = source - capacity[None, :, :, None] * (iterate - previous) - within - couple(iterate, tile_links, conductance)
    log_alpha = math.log(circulant_alpha)
    step_index = jnp.arange(STEPS).astype(jnp.float32)
    weights = jnp.exp(step_index * (log_alpha / STEPS))[:, None, None, None]
    spectrum = jnp.fft.fft(residual * weights, axis=0)
    spec_real = jnp.real(spectrum)
    spec_imag = jnp.imag(spectrum)
    theta = 2.0 * math.pi * step_index / STEPS
    radius = math.exp(log_alpha / STEPS)
    lam_real = 1.0 - radius * jnp.cos(theta)
    lam_imag = radius * jnp.sin(theta)
    shift_real = capacity[None] * lam_real[:, None, None]
    shift_imag = capacity[None] * lam_imag[:, None, None]
    first_real, first_imag = spectral_solve(spec_real, spec_imag, tile_basis, tile_values, shift_real, shift_imag)
    rhs_real = spec_real - couple(first_real, tile_links, conductance)
    rhs_imag = spec_imag - couple(first_imag, tile_links, conductance)
    second_real, second_imag = spectral_solve(rhs_real, rhs_imag, tile_basis, tile_values, shift_real, shift_imag)
    back = jnp.real(jnp.fft.ifft(second_real + 1j * second_imag, axis=0))
    return iterate + back / weights
```

```python
import math

import jax
import jax.numpy as jnp
from jax import lax
from jax.experimental import pallas as pl
from jax.experimental.pallas import tpu as pltpu
from jax.sharding import PartitionSpec as P

ALPHA = 0.05
HIGHEST = lax.Precision.HIGHEST
STEPS = 32
BLOCKS = 32
TILE = 128
PACK = 40
VECS = 9
f32 = jnp.float32


def mm(x, y):
    return jnp.dot(x, y, precision=HIGHEST, preferred_element_type=f32)


def mm_nt(x, y):
    return lax.dot_general(x, y, (((1,), (1,)), ((), ())), precision=HIGHEST, preferred_element_type=f32)


def mm_tn(x, y):
    return lax.dot_general(x, y, (((0,), (0,)), ((), ())), precision=HIGHEST, preferred_element_type=f32)


def rows_of(shape):
    return lax.broadcasted_iota(jnp.int32, shape, 0)


def shift_down(x, by):
    return jnp.where(rows_of(x.shape) >= by, pltpu.roll(x, by, 0), 0.0)


def recurrence(x, decay):
    for by in (1, 2, 4, 8, 16):
        x = x + decay * shift_down(x, by)
        decay = decay * decay
    return x


def power_rows(decay, first, reverse=False):
    n = rows_of((STEPS, TILE))
    exponent = (STEPS - 1 - n if reverse else n) + first
    out = jnp.ones((STEPS, TILE), f32)
    for bit in range(6):
        out = out * jnp.where((exponent >> bit) & 1 == 1, decay, 1.0)
        decay = decay * decay
    return out


def to_32(decay):
    for _ in range(5):
        decay = decay * decay
    return decay


def picked(x, index_row):
    return jnp.take_along_axis(x, jnp.broadcast_to(index_row, x.shape), axis=1, mode="promise_in_bounds")


def params(values_ref, cap_ref, p):
    total = values_ref[p : p + 1, :] + cap_ref[0, p]
    gain = 1.0 / total
    return cap_ref[0, p] * gain, gain


def coupled(p, low, high, own, side, links_ref, cond_ref, col):
    left = jnp.where(col == 1, side[1], 0.0) if p == 0 else own[0]
    right = own[1] if p == 0 else jnp.where(col == 0, side[0], 0.0)
    total = None
    for d, x in enumerate((low[p], high[p], left, right)):
        r = 2 * d + p
        term = cond_ref[r : r + 1, :] * picked(x, links_ref[r : r + 1, :])
        total = term if total is None else total + term
    return total


def every_other(ref, p, start=0):
    return ref[pl.ds(start + p, STEPS, stride=2), :]


def kernel_a(it, src, low, high, side, bas, values, links, cond, init, cap, out):
    col = lax.axis_index("cols")
    block = lax.axis_index("tm")
    pair = lambda ref: (every_other(ref, 0), every_other(ref, 1))
    lows, highs, sides, own = pair(low), pair(high), pair(side), pair(it)
    for p in range(2):
        basis = bas[p * TILE : (p + 1) * TILE, :]
        decay, gain = params(values, cap, p)
        force = every_other(src, p) + coupled(p, lows, highs, own, sides, links, cond, col)
        last = init[p : p + 1, :] - ALPHA * own[p][STEPS - 1 : STEPS, :]
        stacked = jnp.concatenate([force, jnp.broadcast_to(last, (8, TILE))], axis=0)
        modes = mm(stacked, basis)
        wrap = modes[STEPS : STEPS + 1, :]
        state = recurrence(modes[:STEPS] * gain, decay)
        end = state[STEPS - 1 : STEPS, :]
        end = jnp.where(block == BLOCKS - 1, ALPHA * end + wrap, end)
        row = rows_of((8, TILE))
        tail = jnp.where(row == 0, end, jnp.where(row == 1, decay, jnp.where(row == 2, wrap, 0.0)))
        out[p * PACK : p * PACK + STEPS, :] = mm_nt(state, basis)
        out[p * PACK + STEPS : (p + 1) * PACK, :] = tail


def kernel_b(src, own, low, high, side, bas, values, links, cond, cap, local, send):
    col = lax.axis_index("cols")
    block = lax.axis_index("tm")
    pair = lambda ref: (ref[0:STEPS, :], ref[PACK : PACK + STEPS, :])
    lows, highs, sides, owns = pair(low), pair(high), pair(side), pair(own)
    vectors = [ref[p * PACK + STEPS : p * PACK + STEPS + 1, :] for ref in (own, low, high) for p in range(2)]
    ends = [side[p * PACK + STEPS : p * PACK + STEPS + 1, :] for p in range(2)]
    vectors.append(jnp.where(col == 0, ends[0], ends[1]))
    for p in range(2):
        basis = bas[p * TILE : (p + 1) * TILE, :]
        decay, gain = params(values, cap, p)
        force = every_other(src, p) + coupled(p, lows, highs, owns, sides, links, cond, col)
        state = recurrence(mm(force, basis) * gain, decay)
        local[p * STEPS : (p + 1) * STEPS, :] = state
        end = state[STEPS - 1 : STEPS, :]
        wrap = own[p * PACK + STEPS + 2 : p * PACK + STEPS + 3, :]
        vectors.append(jnp.where(block == BLOCKS - 1, ALPHA * end + wrap, end))
    for k, vector in enumerate(vectors):
        send[pl.ds(k, BLOCKS, stride=VECS), :] = jnp.broadcast_to(vector, (BLOCKS, TILE))


def kernel_m(bas, low, high, side, own2, low2, high2, side2, values, links, cond, cap, direct, through, decays):
    col = lax.axis_index("cols")
    at = lambda ref, p: ref[p * PACK + STEPS + 1 : p * PACK + STEPS + 2, :]
    base = lambda ref, p: ref[2 * STEPS + p * TILE : 2 * STEPS + (p + 1) * TILE, :]
    side_decay = jnp.where(col == 0, at(side2, 0), at(side2, 1))
    side_basis = jnp.where(col == 0, base(side, 0), base(side, 1))
    rows = [at(own2, 0), at(own2, 1), at(low2, 0), at(low2, 1), at(high2, 0), at(high2, 1), side_decay, side_decay]
    for k, row in enumerate(rows):
        decays[k : k + 1, :] = row
    table = [power_rows(row, 1) for row in rows[:7]]
    node = rows_of((TILE, TILE))
    for p in range(2):
        basis = bas[p * TILE : (p + 1) * TILE, :]
        decay, gain = params(values, cap, p)
        own_table = power_rows(decay, 0, reverse=True) * gain
        outside = jnp.where(col == (1 if p == 0 else 0), 1.0, 0.0)
        other = bas[(1 - p) * TILE : (2 - p) * TILE, :]
        slots = [(base(low, p), table[2 + p], None), (base(high, p), table[4 + p], None)]
        inner, outer = (other, table[1 - p], None), (side_basis, table[6], outside)
        slots += [outer, inner] if p == 0 else [inner, outer]
        for d, (neighbour, its_table, mask) in enumerate(slots):
            r = 2 * d + p
            weight = cond[r : r + 1, :] if mask is None else cond[r : r + 1, :] * mask
            ties = jnp.where(links[r : r + 1, :] == node, weight, 0.0)
            matrix = mm_tn(neighbour, mm(ties, basis))
            at_row = (p * 4 + d) * TILE
            direct[at_row : at_row + TILE, :] = matrix
            through[at_row : at_row + TILE, :] = matrix * mm_tn(its_table, own_table)


def incoming(ends, decay):
    block_decay = to_32(decay)
    summed = recurrence(ends, block_decay)
    start = (ALPHA * block_decay * summed[BLOCKS - 2 : BLOCKS - 1, :] + ends[BLOCKS - 1 : BLOCKS, :]) / (
        1.0 - ALPHA * to_32(block_decay)
    )
    return shift_down(summed, 1) + power_rows(block_decay, 0) * start


def row_at(x, index):
    return jnp.sum(jnp.where(rows_of(x.shape) == index, x, 0.0), axis=0, keepdims=True)


def kernel_c(received, local, direct, through, decays, bas, values, cap, out):
    block = lax.axis_index("tm")
    vector = lambda k: received[pl.ds(k, BLOCKS, stride=VECS), :]
    states, paths = [], []
    for k in range(7):
        decay = decays[k : k + 1, :]
        state = incoming(vector(k), decay)
        states.append(state)
        paths.append(power_rows(decay, 1) * row_at(state, block))
    factor = jnp.where(rows_of((BLOCKS, TILE)) == BLOCKS - 1, ALPHA, 1.0)
    for p in range(2):
        order = (2, 4, 6, 1) if p == 0 else (3, 5, 0, 6)
        basis = bas[p * TILE : (p + 1) * TILE, :]
        decay, gain = params(values, cap, p)
        span = slice(p * 4 * TILE, (p + 1) * 4 * TILE)
        added = mm(jnp.concatenate([states[k] for k in order], axis=1), through[span, :])
        ends = vector(7 + p) + factor * added
        entering = row_at(incoming(ends, decay), block)
        force = mm(jnp.concatenate([paths[k] for k in order], axis=1), direct[span, :])
        state = local[p * STEPS : (p + 1) * STEPS, :] + recurrence(force * gain, decay)
        state = state + power_rows(decay, 1) * entering
        out[pl.ds(p, STEPS, stride=2), :] = mm_nt(state, basis)


def call(kernel, outs, *args):
    vmem = pl.BlockSpec(memory_space=pltpu.VMEM)
    smem = pl.BlockSpec(memory_space=pltpu.SMEM)
    shapes = [jax.ShapeDtypeStruct(shape, f32) for shape in outs]
    single = len(outs) == 1
    return pl.pallas_call(
        kernel,
        out_shape=shapes[0] if single else shapes,
        in_specs=[smem if arg.shape == (1, 2) else vmem for arg in args],
        out_specs=vmem if single else [vmem] * len(outs),
    )(*args)


def around(x):
    count = lax.axis_size("rows")
    up = [(i, i + 1) for i in range(count - 1)]
    low = lax.ppermute(x, "rows", up)
    high = lax.ppermute(x, "rows", [(b, a) for a, b in up])
    side = lax.ppermute(x, "cols", [(0, 1), (1, 0)])
    return low, high, side


def on_device(iterate, source, initial, tile_basis, tile_values, capacity, tile_links, conductance):
    it = iterate.reshape(2 * STEPS, TILE)
    src = source.reshape(2 * STEPS, TILE)
    init = initial.reshape(2, TILE)
    bas = tile_basis.reshape(2 * TILE, TILE)
    values = tile_values.reshape(2, TILE)
    links = tile_links.reshape(8, TILE)
    cond = conductance.reshape(8, TILE)
    first = around(jnp.concatenate([it, bas], axis=0))
    own2 = call(kernel_a, [(2 * PACK, TILE)], it, src, *first, bas, values, links, cond, init, capacity)
    second = around(own2)
    local, send = call(
        kernel_b, [(2 * STEPS, TILE), (BLOCKS * VECS, TILE)], src, own2, *second, bas, values, links, cond, capacity
    )
    direct, through, decays = call(
        kernel_m,
        [(8 * TILE, TILE), (8 * TILE, TILE), (8, TILE)],
        bas, *first, own2, *second, values, links, cond, capacity,
    )
    flat = send.reshape(BLOCKS, VECS * TILE)
    received = lax.all_to_all(flat, "tm", split_axis=0, concat_axis=0, tiled=True).reshape(BLOCKS * VECS, TILE)
    out = call(kernel_c, [(2 * STEPS, TILE)], received, local, direct, through, decays, bas, values, capacity)
    return out.reshape(iterate.shape)


def solution(mesh):
    in_specs = (
        P("tm", "rows", "cols", None),
        P("tm", "rows", "cols", None),
        P("rows", "cols", None),
        P("rows", "cols", None, None),
        P("rows", "cols", None),
        P("rows", "cols"),
        P(None, "rows", "cols", None),
        P(None, "rows", "cols", None),
    )
    out_specs = P("tm", "rows", "cols", None)
    return jax.shard_map(on_device, mesh=mesh, in_specs=in_specs, out_specs=out_specs, check_vma=False)
```

```python
import math

import jax
import jax.numpy as jnp
from jax import lax
from jax.experimental import pallas as pl
from jax.experimental.pallas import tpu as pltpu
from jax.sharding import PartitionSpec as P

ALPHA = 0.05
HIGHEST = lax.Precision.HIGHEST
STEPS = 32
BLOCKS = 32
TILE = 128
PACK = 40
VECS = 9
FIRST = 22
TURNED = [(i + FIRST) % BLOCKS for i in range(BLOCKS)]
ROWS2 = 2 * PACK
f32 = jnp.float32


def mm(x, y):
    return jnp.dot(x, y, precision=HIGHEST, preferred_element_type=f32)


def mm_nt(x, y):
    return lax.dot_general(x, y, (((1,), (1,)), ((), ())), precision=HIGHEST, preferred_element_type=f32)


def mm_tn(x, y):
    return lax.dot_general(x, y, (((0,), (0,)), ((), ())), precision=HIGHEST, preferred_element_type=f32)


def rows_of(shape):
    return lax.broadcasted_iota(jnp.int32, shape, 0)


def shift_down(x, by):
    return jnp.where(rows_of(x.shape) >= by, pltpu.roll(x, by, 0), 0.0)


def recurrence(x, decay):
    for by in (1, 2, 4, 8, 16):
        x = x + decay * shift_down(x, by)
        decay = decay * decay
    return x


def power_rows(decay, first, reverse=False):
    n = rows_of((STEPS, TILE))
    exponent = (STEPS - 1 - n if reverse else n) + first
    out = jnp.ones((STEPS, TILE), f32)
    for bit in range(6):
        out = out * jnp.where((exponent >> bit) & 1 == 1, decay, 1.0)
        decay = decay * decay
    return out


def to_32(decay):
    for _ in range(5):
        decay = decay * decay
    return decay


def picked(x, index_row):
    return jnp.take_along_axis(x, jnp.broadcast_to(index_row, x.shape), axis=1, mode="promise_in_bounds")


def params(values_ref, cap_ref, p):
    total = values_ref[p : p + 1, :] + cap_ref[0, p]
    gain = 1.0 / total
    return cap_ref[0, p] * gain, gain


def coupled(p, low, high, own, side, links_ref, cond_ref, col):
    left = jnp.where(col == 1, side, 0.0) if p == 0 else own[0]
    right = own[1] if p == 0 else jnp.where(col == 0, side, 0.0)
    total = None
    for d, x in enumerate((low[p], high[p], left, right)):
        r = 2 * d + p
        term = cond_ref[r : r + 1, :] * picked(x, links_ref[r : r + 1, :])
        total = term if total is None else total + term
    return total


def every_other(ref, p, start=0):
    return ref[pl.ds(start + p, STEPS, stride=2), :]


def kernel_p(it, bas, values, links, cond, init, rows_pack, cols_pack, values_out, links_out, cond_out, init_out):
    col = lax.axis_index("cols")
    rows_pack[0 : 2 * STEPS, :] = it[...]
    rows_pack[2 * STEPS :, :] = bas[...]
    near = 1 - col
    cols_pack[0:STEPS, :] = jnp.where(col == 0, every_other(it, 1), every_other(it, 0))
    cols_pack[STEPS:, :] = bas[pl.ds(pl.multiple_of(near * TILE, TILE), TILE), :]
    values_out[...] = values[...]
    links_out[...] = links[...]
    cond_out[...] = cond[...]
    init_out[...] = init[...]


def kernel_a(it, src, inner, outer, side, bas, values, links, cond, init, cap, out, copies):
    col = lax.axis_index("cols")
    block = lax.axis_index("tm")
    pair = lambda ref: (every_other(ref, 0), every_other(ref, 1))
    sides, own = side[0:STEPS, :], pair(it)
    lows, highs = zip(*(ordered(a, b) for a, b in zip(pair(inner), pair(outer))))
    for p in range(2):
        basis = bas[p * TILE : (p + 1) * TILE, :]
        decay, gain = params(values, cap, p)
        force = every_other(src, p) + coupled(p, lows, highs, own, sides, links, cond, col)
        last = init[p : p + 1, :] - ALPHA * own[p][STEPS - 1 : STEPS, :]
        stacked = jnp.concatenate([force, jnp.broadcast_to(last, (8, TILE))], axis=0)
        modes = mm(stacked, basis)
        wrap = modes[STEPS : STEPS + 1, :]
        state = recurrence(modes[:STEPS] * gain, decay)
        end = state[STEPS - 1 : STEPS, :]
        end = jnp.where(block == BLOCKS - 1, ALPHA * end + wrap, end)
        row = rows_of((8, TILE))
        tail = jnp.where(row == 0, end, jnp.where(row == 1, decay, jnp.where(row == 2, wrap, 0.0)))
        first = mm_nt(state, basis)
        for ref, rows in ((out, ROWS2), (copies, 4 * ROWS2)):
            for at in range(p * PACK, rows, ROWS2):
                ref[at : at + STEPS, :] = first
                ref[at + STEPS : at + PACK, :] = tail


def quad_rows(start, count):
    odd, col = lax.axis_index("rows") % 2, lax.axis_index("cols")
    inner = ((1 - odd) * 2 + col) * ROWS2 + start
    near = jnp.where(col == 0, 0, PACK)
    side = (odd * 2 + 1 - col) * ROWS2 + near + start
    return pl.ds(pl.multiple_of(inner, 8), count), pl.ds(pl.multiple_of(side, 8), count)


def kernel_b(src, own, quad, outer, bas, values, links, cond, cap, local, send):
    col = lax.axis_index("cols")
    block = lax.axis_index("tm")
    both = lambda ref, start, count: [ref[p * PACK + start : p * PACK + start + count, :] for p in range(2)]
    inner = lambda start, count: [quad[quad_rows(p * PACK + start, count)[0], :] for p in range(2)]
    side = lambda start, count: quad[quad_rows(start, count)[1], :]
    owns, sides = both(own, 0, STEPS), side(0, STEPS)
    lows, highs = zip(*(ordered(a, b) for a, b in zip(inner(0, STEPS), both(outer, 0, STEPS))))
    low_ends, high_ends = zip(*(ordered(a, b) for a, b in zip(inner(STEPS, 8), both(outer, STEPS, 8))))
    vectors = [x[0:1, :] for x in (*both(own, STEPS, 8), *low_ends, *high_ends, side(STEPS, 8))]
    for p in range(2):
        basis = bas[p * TILE : (p + 1) * TILE, :]
        decay, gain = params(values, cap, p)
        force = every_other(src, p) + coupled(p, lows, highs, owns, sides, links, cond, col)
        state = recurrence(mm(force, basis) * gain, decay)
        local[p * STEPS : (p + 1) * STEPS, :] = state
        end = state[STEPS - 1 : STEPS, :]
        wrap = own[p * PACK + STEPS + 2 : p * PACK + STEPS + 3, :]
        vectors.append(jnp.where(block == BLOCKS - 1, ALPHA * end + wrap, end))
    for k, vector in enumerate(vectors):
        send[pl.ds(k, BLOCKS, stride=VECS), :] = jnp.broadcast_to(vector, (BLOCKS, TILE))


def kernel_m(bas, inner, outer, side, own2, quad, outer2, values, links, cond, cap, direct, through, decays):
    col = lax.axis_index("cols")
    at = lambda ref, p: ref[p * PACK + STEPS : p * PACK + STEPS + 8, :][1:2, :]
    base = lambda ref, p: ref[2 * STEPS + p * TILE : 2 * STEPS + (p + 1) * TILE, :]
    side_decay = quad[quad_rows(STEPS, 8)[1], :][1:2, :]
    side_basis = side[STEPS : STEPS + TILE, :]
    inner_decay = [quad[quad_rows(p * PACK + STEPS, 8)[0], :][1:2, :] for p in range(2)]
    low_decay, high_decay = zip(*(ordered(inner_decay[p], at(outer2, p)) for p in range(2)))
    rows = [at(own2, 0), at(own2, 1), *low_decay, *high_decay, side_decay, side_decay]
    for k, row in enumerate(rows):
        decays[k : k + 1, :] = row
    table = [power_rows(row, 1) for row in rows[:7]]
    node = rows_of((TILE, TILE))
    for p in range(2):
        basis = bas[p * TILE : (p + 1) * TILE, :]
        decay, gain = params(values, cap, p)
        own_table = power_rows(decay, 0, reverse=True) * gain
        outside = jnp.where(col == (1 if p == 0 else 0), 1.0, 0.0)
        other = bas[(1 - p) * TILE : (2 - p) * TILE, :]
        low, high = ordered(base(inner, p), base(outer, p))
        slots = [(low, table[2 + p], None), (high, table[4 + p], None)]
        near, far = (other, table[1 - p], None), (side_basis, table[6], outside)
        slots += [far, near] if p == 0 else [near, far]
        for d, (neighbour, its_table, mask) in enumerate(slots):
            r = 2 * d + p
            weight = cond[r : r + 1, :] if mask is None else cond[r : r + 1, :] * mask
            ties = jnp.where(links[r : r + 1, :] == node, weight, 0.0)
            matrix = mm_tn(neighbour, mm(ties, basis))
            at_row = (p * 4 + d) * TILE
            direct[at_row : at_row + TILE, :] = matrix
            through[at_row : at_row + TILE, :] = matrix * mm_tn(its_table, own_table)


def incoming(ends, decay):
    block_decay = to_32(decay)
    summed = recurrence(ends, block_decay)
    start = (ALPHA * block_decay * summed[BLOCKS - 2 : BLOCKS - 1, :] + ends[BLOCKS - 1 : BLOCKS, :]) / (
        1.0 - ALPHA * to_32(block_decay)
    )
    return shift_down(summed, 1) + power_rows(block_decay, 0) * start


def row_at(x, index):
    return jnp.sum(jnp.where(rows_of(x.shape) == index, x, 0.0), axis=0, keepdims=True)


def kernel_c(received, local, direct, through, decays, bas, values, cap, out):
    block = lax.axis_index("tm")
    vector = lambda k: pltpu.roll(received[pl.ds(k, BLOCKS, stride=VECS), :], FIRST, 0)
    states, paths = [], []
    for k in range(7):
        decay = decays[k : k + 1, :]
        state = incoming(vector(k), decay)
        states.append(state)
        paths.append(power_rows(decay, 1) * row_at(state, block))
    factor = jnp.where(rows_of((BLOCKS, TILE)) == BLOCKS - 1, ALPHA, 1.0)
    for p in range(2):
        order = (2, 4, 6, 1) if p == 0 else (3, 5, 0, 6)
        basis = bas[p * TILE : (p + 1) * TILE, :]
        decay, gain = params(values, cap, p)
        span = slice(p * 4 * TILE, (p + 1) * 4 * TILE)
        added = mm(jnp.concatenate([states[k] for k in order], axis=1), through[span, :])
        ends = vector(7 + p) + factor * added
        entering = row_at(incoming(ends, decay), block)
        force = mm(jnp.concatenate([paths[k] for k in order], axis=1), direct[span, :])
        state = local[p * STEPS : (p + 1) * STEPS, :] + recurrence(force * gain, decay)
        state = state + power_rows(decay, 1) * entering
        out[pl.ds(p, STEPS, stride=2), :] = mm_nt(state, basis)


def call(kernel, outs, *args, last=False, plain=False):
    vmem = pl.BlockSpec(memory_space=pltpu.VMEM)
    smem = pl.BlockSpec(memory_space=pltpu.SMEM)
    outs = [out if isinstance(out[0], tuple) else (out, f32) for out in outs]
    shapes = [jax.ShapeDtypeStruct(*out) if last else pltpu.VMEM(*out) for out in outs]
    single = len(outs) == 1
    scalar = lambda arg: arg.shape == (1, 2)
    near = lambda arg: arg if plain or scalar(arg) else pltpu.with_memory_space_constraint(arg, pltpu.VMEM)
    return pl.pallas_call(
        kernel,
        out_shape=shapes[0] if single else shapes,
        in_specs=[smem if scalar(arg) else vmem for arg in args],
        out_specs=vmem if single else [vmem] * len(outs),
    )(*[near(arg) for arg in args])


def swaps(first):
    return [pair for i in range(first, lax.axis_size("rows") - 1, 2) for pair in ((i, i + 1), (i + 1, i))]


def ordered(inner, outer):
    odd = lax.axis_index("rows") % 2 == 1
    return jnp.where(odd, inner, outer), jnp.where(odd, outer, inner)


def on_device(iterate, source, initial, tile_basis, tile_values, capacity, tile_links, conductance):
    it = iterate.reshape(2 * STEPS, TILE)
    src = source.reshape(2 * STEPS, TILE)
    init = initial.reshape(2, TILE)
    bas = tile_basis.reshape(2 * TILE, TILE)
    values = tile_values.reshape(2, TILE)
    links = tile_links.reshape(8, TILE)
    cond = conductance.reshape(8, TILE)
    rows_pack, cols_pack, values, links, cond, init = call(
        kernel_p,
        [(2 * STEPS + 2 * TILE, TILE), (STEPS + TILE, TILE), (2, TILE), ((8, TILE), jnp.int32), (8, TILE), (2, TILE)],
        it, bas, values, links, cond, init, plain=True,
    )
    inner = lax.ppermute(rows_pack, "rows", swaps(0))
    outer = lax.ppermute(rows_pack, "rows", swaps(1))
    side = lax.ppermute(cols_pack, "cols", [(0, 1), (1, 0)])
    own2, copies = call(
        kernel_a, [(ROWS2, TILE), (4 * ROWS2, TILE)], it, src, inner, outer, side, bas, values, links, cond, init, capacity
    )
    fours = [[4 * k + j for j in range(4)] for k in range(lax.axis_size("rows") // 2)]
    quad = lax.all_to_all(
        copies.reshape(4, ROWS2, TILE), ("rows", "cols"), split_axis=0, concat_axis=0, tiled=True,
        axis_index_groups=fours,
    ).reshape(4 * ROWS2, TILE)
    outer2 = lax.ppermute(own2, "rows", swaps(1))
    local, send = call(
        kernel_b, [(2 * STEPS, TILE), (BLOCKS * VECS, TILE)], src, own2, quad, outer2, bas, values, links, cond, capacity
    )
    direct, through, decays = call(
        kernel_m,
        [(8 * TILE, TILE), (8 * TILE, TILE), (8, TILE)],
        bas, inner, outer, side, own2, quad, outer2, values, links, cond, capacity,
    )
    flat = send.reshape(BLOCKS, VECS * TILE)
    received = lax.all_to_all(
        flat, "tm", split_axis=0, concat_axis=0, tiled=True, axis_index_groups=[TURNED]
    ).reshape(BLOCKS * VECS, TILE)
    out = call(kernel_c, [(2 * STEPS, TILE)], received, local, direct, through, decays, bas, values, capacity, last=True)
    return out.reshape(iterate.shape)


def solution(mesh):
    in_specs = (
        P("tm", "rows", "cols", None),
        P("tm", "rows", "cols", None),
        P("rows", "cols", None),
        P("rows", "cols", None, None),
        P("rows", "cols", None),
        P("rows", "cols"),
        P(None, "rows", "cols", None),
        P(None, "rows", "cols", None),
    )
    out_specs = P("tm", "rows", "cols", None)
    return jax.shard_map(on_device, mesh=mesh, in_specs=in_specs, out_specs=out_specs, check_vma=False)
```

```python
import jax
import jax.numpy as jnp
from jax import lax
from jax.experimental import pallas as pl
from jax.experimental.pallas import tpu as pltpu
from jax.sharding import PartitionSpec as P


ALPHA = 0.05
HIGHEST = lax.Precision.HIGHEST
STEPS = 32
BLOCKS = 32
TILE = 128
PACK = 40
VECS = 9
FIRST = 22
TURNED = [(i + FIRST) % BLOCKS for i in range(BLOCKS)]
ROWS2 = 2 * PACK
f32 = jnp.float32


def mm(x, y):
    return jnp.dot(x, y, precision=HIGHEST, preferred_element_type=f32)


def mm_nt(x, y):
    return lax.dot_general(x, y, (((1,), (1,)), ((), ())), precision=HIGHEST, preferred_element_type=f32)


def mm_tn(x, y):
    return lax.dot_general(x, y, (((0,), (0,)), ((), ())), precision=HIGHEST, preferred_element_type=f32)


def rows_of(shape):
    return lax.broadcasted_iota(jnp.int32, shape, 0)


def shift_down(x, by):
    return jnp.where(rows_of(x.shape) >= by, pltpu.roll(x, by, 0), 0.0)


def recurrence(x, decay):
    for by in (1, 2, 4, 8, 16):
        x = x + decay * shift_down(x, by)
        decay = decay * decay
    return x


def power_rows(decay, first, reverse=False):
    n = rows_of((STEPS, TILE))
    exponent = (STEPS - 1 - n if reverse else n) + first
    out = jnp.ones((STEPS, TILE), f32)
    for bit in range(6):
        out = out * jnp.where((exponent >> bit) & 1 == 1, decay, 1.0)
        decay = decay * decay
    return out


def to_32(decay):
    for _ in range(5):
        decay = decay * decay
    return decay


def picked(x, index_row):
    return jnp.take_along_axis(x, jnp.broadcast_to(index_row, x.shape), axis=1, mode="promise_in_bounds")


def params(values_ref, cap_ref, p):
    total = values_ref[p : p + 1, :] + cap_ref[0, p]
    gain = 1.0 / total
    return cap_ref[0, p] * gain, gain


def coupled(p, low, high, own, side, links_ref, cond_ref, col):
    left = jnp.where(col == 1, side, 0.0) if p == 0 else own[0]
    right = own[1] if p == 0 else jnp.where(col == 0, side, 0.0)
    total = None
    for d, x in enumerate((low[p], high[p], left, right)):
        r = 2 * d + p
        term = cond_ref[r : r + 1, :] * picked(x, links_ref[r : r + 1, :])
        total = term if total is None else total + term
    return total


def every_other(ref, p, start=0):
    return ref[pl.ds(start + p, STEPS, stride=2), :]


def kernel_p(it, values, links, cond, init, copies, own, values_out, links_out, cond_out, init_out):
    own[...] = it[...]
    for k in range(4):
        copies[k * 2 * STEPS : (k + 1) * 2 * STEPS, :] = it[...]
    values_out[...] = values[...]
    links_out[...] = links[...]
    cond_out[...] = cond[...]
    init_out[...] = init[...]


def prepare(it, *small):
    vmem = pl.BlockSpec(memory_space=pltpu.VMEM)
    return pl.pallas_call(
        kernel_p,
        out_shape=[
            jax.ShapeDtypeStruct((8 * STEPS, TILE), f32),
            pltpu.VMEM(it.shape, f32),
            *[pltpu.VMEM(x.shape, x.dtype) for x in small],
        ],
        in_specs=[vmem] * (len(small) + 1),
        out_specs=[vmem] * (len(small) + 2),
    )(it, *small)


def quad_rows(start, count, height):
    odd, col = lax.axis_index("rows") % 2, lax.axis_index("cols")
    inner = ((1 - odd) * 2 + col) * 2 * height + start
    side = (odd * 2 + 1 - col) * 2 * height + jnp.where(col == 0, 0, height) + start
    return pl.ds(pl.multiple_of(inner, 8), count), pl.ds(pl.multiple_of(side, 8), count)


def kernel_a(it, src, quad, outer, bas, values, links, cond, init, cap, out, copies, near_basis):
    col = lax.axis_index("cols")
    block = lax.axis_index("tm")
    near_basis[...] = bas[pl.ds(pl.multiple_of((1 - col) * TILE, TILE), TILE), :]
    pair = lambda ref: [every_other(ref, p) for p in range(2)]
    chunk = lambda k: [every_other(quad, p, pl.multiple_of(k * 2 * STEPS, 2 * STEPS)) for p in range(2)]
    odd = lax.axis_index("rows") % 2
    inner, across, own = chunk((1 - odd) * 2 + col), chunk(odd * 2 + 1 - col), pair(it)
    sides = jnp.where(col == 0, across[0], across[1])
    lows, highs = zip(*(ordered(a, b) for a, b in zip(inner, pair(outer))))
    for p in range(2):
        basis = bas[p * TILE : (p + 1) * TILE, :]
        decay, gain = params(values, cap, p)
        force = every_other(src, p) + coupled(p, lows, highs, own, sides, links, cond, col)
        last = init[p : p + 1, :] - ALPHA * own[p][STEPS - 1 : STEPS, :]
        stacked = jnp.concatenate([force, jnp.broadcast_to(last, (8, TILE))], axis=0)
        modes = mm(stacked, basis)
        wrap = modes[STEPS : STEPS + 1, :]
        state = recurrence(modes[:STEPS] * gain, decay)
        end = state[STEPS - 1 : STEPS, :]
        end = jnp.where(block == BLOCKS - 1, ALPHA * end + wrap, end)
        row = rows_of((8, TILE))
        tail = jnp.where(row == 0, end, jnp.where(row == 1, decay, jnp.where(row == 2, wrap, 0.0)))
        first = mm_nt(state, basis)
        for ref, rows in ((out, ROWS2), (copies, 4 * ROWS2)):
            for at in range(p * PACK, rows, ROWS2):
                ref[at : at + STEPS, :] = first
                ref[at + STEPS : at + PACK, :] = tail


def kernel_b(src, own, quad, outer, bas, values, links, cond, cap, local, send):
    col = lax.axis_index("cols")
    block = lax.axis_index("tm")
    both = lambda ref, start, count: [ref[p * PACK + start : p * PACK + start + count, :] for p in range(2)]
    inner = lambda start, count: [quad[quad_rows(p * PACK + start, count, PACK)[0], :] for p in range(2)]
    side = lambda start, count: quad[quad_rows(start, count, PACK)[1], :]
    owns, sides = both(own, 0, STEPS), side(0, STEPS)
    lows, highs = zip(*(ordered(a, b) for a, b in zip(inner(0, STEPS), both(outer, 0, STEPS))))
    ends = (*both(own, STEPS, 8), *both(outer, STEPS, 8), *inner(STEPS, 8), side(STEPS, 8))
    vectors = [x[0:1, :] for x in ends]
    for p in range(2):
        basis = bas[p * TILE : (p + 1) * TILE, :]
        decay, gain = params(values, cap, p)
        force = every_other(src, p) + coupled(p, lows, highs, owns, sides, links, cond, col)
        state = recurrence(mm(force, basis) * gain, decay)
        local[p * STEPS : (p + 1) * STEPS, :] = state
        end = state[STEPS - 1 : STEPS, :]
        wrap = own[p * PACK + STEPS + 2 : p * PACK + STEPS + 3, :]
        vectors.append(jnp.where(block == BLOCKS - 1, ALPHA * end + wrap, end))
    for k, vector in enumerate(vectors):
        send[pl.ds(k, BLOCKS, stride=VECS), :] = jnp.broadcast_to(vector, (BLOCKS, TILE))


def matrices(p, neighbour, table, tie_rows, mask, bas, values, cap):
    basis = bas[p * TILE : (p + 1) * TILE, :]
    decay, gain = params(values, cap, p)
    link, weight = tie_rows
    weight = weight if mask is None else weight * mask
    direct = mm(weight * picked(neighbour.T, link), basis)
    return direct, direct * mm_tn(table, power_rows(decay, 0, reverse=True) * gain)


def ties_of(links, cond, low, high, odd):
    pick = lambda ref: jnp.where(odd, ref[high : high + 1, :], ref[low : low + 1, :])
    return pick(links), pick(cond)


def kernel_m(bas, outer, own2, quad, outer2, values, links, cond, cap, direct, through, tables, decays):
    odd = lax.axis_index("rows") % 2 == 1
    at = lambda x: x[1:2, :]
    both = lambda ref: [ref[p * PACK + STEPS : (p + 1) * PACK, :] for p in range(2)]
    inner = [quad[quad_rows(p * PACK + STEPS, 8, PACK)[0], :] for p in range(2)]
    side = quad[quad_rows(STEPS, 8, PACK)[1], :]
    for k, x in enumerate((*both(own2), *both(outer2), *inner, side)):
        decay = at(x)
        block_decay = to_32(decay)
        scale = 1.0 / (1.0 - ALPHA * to_32(block_decay))
        decays[k : k + 1, :] = block_decay
        tables[k * STEPS : (k + 1) * STEPS, :] = power_rows(decay, 1)
        tables[(7 + k) * STEPS : (8 + k) * STEPS, :] = power_rows(block_decay, 0) * scale
    decays[7:8, :] = jnp.zeros((1, TILE), f32)
    table = lambda k: tables[k * STEPS : (k + 1) * STEPS, :]
    for p in range(2):
        tile = lambda ref, q: ref[q * TILE : (q + 1) * TILE, :]
        near = 2 * (3 - p) + p
        for j, (neighbour, k, ties) in enumerate((
            (tile(outer, p), 2 + p, ties_of(links, cond, p, 2 + p, odd)),
            (tile(bas, 1 - p), 1 - p, ties_of(links, cond, near, near, odd)),
        )):
            rows = slice((2 * p + j) * TILE, (2 * p + j + 1) * TILE)
            direct[rows, :], through[rows, :] = matrices(p, neighbour, table(k), ties, None, bas, values, cap)


def kernel_n(bas, inner, side, tables, values, links, cond, cap, direct, through):
    odd = lax.axis_index("rows") % 2 == 1
    col = lax.axis_index("cols")
    table = lambda k: tables[k * STEPS : (k + 1) * STEPS, :]
    for p in range(2):
        far = 2 * (2 + p) + p
        outside = jnp.where(col == 1 - p, 1.0, 0.0)
        for j, (neighbour, k, ties, mask) in enumerate((
            (inner[p * TILE : (p + 1) * TILE, :], 4 + p, ties_of(links, cond, 2 + p, p, odd), None),
            (side[...], 6, ties_of(links, cond, far, far, odd), outside),
        )):
            rows = slice((2 * p + j) * TILE, (2 * p + j + 1) * TILE)
            direct[rows, :], through[rows, :] = matrices(p, neighbour, table(k), ties, mask, bas, values, cap)


def incoming(ends, block_decay, scaled_powers):
    summed = recurrence(ends, block_decay)
    start = ALPHA * block_decay * summed[BLOCKS - 2 : BLOCKS - 1, :] + ends[BLOCKS - 1 : BLOCKS, :]
    return shift_down(summed, 1) + scaled_powers * start


def row_at(x, index):
    return jnp.sum(jnp.where(rows_of(x.shape) == index, x, 0.0), axis=0, keepdims=True)


def kernel_c(received, local, direct1, through1, direct2, through2, tables, decays, bas, values, cap, out):
    block = lax.axis_index("tm")
    vector = lambda k: pltpu.roll(received[pl.ds(k, BLOCKS, stride=VECS), :], FIRST, 0)
    table = lambda k: tables[k * STEPS : (k + 1) * STEPS, :]
    states = [incoming(vector(k), decays[k : k + 1, :], table(7 + k)) for k in range(7)]
    paths = [table(k) * row_at(states[k], block) for k in range(7)]
    factor = jnp.where(rows_of((BLOCKS, TILE)) == BLOCKS - 1, ALPHA, 1.0)
    for p in range(2):
        basis = bas[p * TILE : (p + 1) * TILE, :]
        decay, gain = params(values, cap, p)
        span = slice(2 * p * TILE, 2 * (p + 1) * TILE)
        beside = lambda x, j, k: jnp.concatenate([x[j], x[k]], axis=1)
        product = lambda x, first, second: mm(beside(x, 2 + p, 1 - p), first[span, :]) + mm(
            beside(x, 4 + p, 6), second[span, :]
        )
        ends = vector(7 + p) + factor * product(states, through1, through2)
        entering = row_at(incoming(ends, decays[p : p + 1, :], table(7 + p)), block)
        force = product(paths, direct1, direct2)
        state = local[p * STEPS : (p + 1) * STEPS, :] + recurrence(force * gain, decay)
        state = state + table(p) * entering
        out[pl.ds(p, STEPS, stride=2), :] = mm_nt(state, basis)


def call(kernel, outs, *args, last=False):
    vmem = pl.BlockSpec(memory_space=pltpu.VMEM)
    smem = pl.BlockSpec(memory_space=pltpu.SMEM)
    shapes = [jax.ShapeDtypeStruct(out, f32) if last else pltpu.VMEM(out, f32) for out in outs]
    single = len(outs) == 1
    scalar = lambda arg: arg.shape == (1, 2)
    near = lambda arg: arg if scalar(arg) else pltpu.with_memory_space_constraint(arg, pltpu.VMEM)
    return pl.pallas_call(
        kernel,
        out_shape=shapes[0] if single else shapes,
        in_specs=[smem if scalar(arg) else vmem for arg in args],
        out_specs=vmem if single else [vmem] * len(outs),
    )(*[near(arg) for arg in args])


def swaps(first):
    return [pair for i in range(first, lax.axis_size("rows") - 1, 2) for pair in ((i, i + 1), (i + 1, i))]


def ordered(inner, outer):
    odd = lax.axis_index("rows") % 2 == 1
    return jnp.where(odd, inner, outer), jnp.where(odd, outer, inner)


def on_device(iterate, source, initial, tile_basis, tile_values, capacity, tile_links, conductance):
    it = iterate.reshape(2 * STEPS, TILE)
    src = source.reshape(2 * STEPS, TILE)
    init = initial.reshape(2, TILE)
    bas = tile_basis.reshape(2 * TILE, TILE)
    values = tile_values.reshape(2, TILE)
    links = tile_links.reshape(8, TILE)
    cond = conductance.reshape(8, TILE)
    copies, own, values, links, cond, init = prepare(it, values, links, cond, init)
    fours = [[4 * k + j for j in range(4)] for k in range(lax.axis_size("rows") // 2)]

    def exchange(own, copies):
        quad = lax.all_to_all(
            copies.reshape(4, *own.shape), ("rows", "cols"), split_axis=0, concat_axis=0, tiled=True,
            axis_index_groups=fours,
        )
        return quad.reshape(copies.shape), lax.ppermute(own, "rows", swaps(1))

    quad1, outer1 = exchange(own, copies)
    outer_basis = lax.ppermute(bas, "rows", swaps(1))
    own2, copies2, near_basis = call(
        kernel_a,
        [(ROWS2, TILE), (4 * ROWS2, TILE), (TILE, TILE)],
        own, src, quad1, outer1, bas, values, links, cond, init, capacity,
    )
    quad, outer2 = exchange(own2, copies2)
    rows_basis, _ = lax.optimization_barrier((bas, own2))
    inner_basis = lax.ppermute(rows_basis, "rows", swaps(0))
    local, send = call(
        kernel_b,
        [(2 * STEPS, TILE), (BLOCKS * VECS, TILE)],
        src, own2, quad, outer2, bas, values, links, cond, capacity,
    )
    flat = send.reshape(BLOCKS, VECS * TILE)
    received = lax.all_to_all(
        flat, "tm", split_axis=0, concat_axis=0, tiled=True, axis_index_groups=[TURNED]
    ).reshape(BLOCKS * VECS, TILE)
    near_basis, _ = lax.optimization_barrier((near_basis, send))
    side_basis = lax.ppermute(near_basis, "cols", [(0, 1), (1, 0)])
    pair_shape, table_shape = (4 * TILE, TILE), (14 * STEPS, TILE)
    direct1, through1, tables, decays = call(
        kernel_m,
        [pair_shape, pair_shape, table_shape, (8, TILE)],
        bas, outer_basis, own2, quad, outer2, values, links, cond, capacity,
    )
    direct2, through2 = call(
        kernel_n, [pair_shape, pair_shape], bas, inner_basis, side_basis, tables, values, links, cond, capacity
    )
    out = call(kernel_c, [(2 * STEPS, TILE)], received, local, direct1, through1, direct2, through2, tables, decays, bas, values, capacity, last=True)
    return out.reshape(iterate.shape)


def solution(mesh):
    in_specs = (
        P("tm", "rows", "cols", None),
        P("tm", "rows", "cols", None),
        P("rows", "cols", None),
        P("rows", "cols", None, None),
        P("rows", "cols", None),
        P("rows", "cols"),
        P(None, "rows", "cols", None),
        P(None, "rows", "cols", None),
    )
    out_specs = P("tm", "rows", "cols", None)
    return jax.shard_map(on_device, mesh=mesh, in_specs=in_specs, out_specs=out_specs, check_vma=False)
```

```python
import jax
import jax.numpy as jnp
from jax import lax
from jax.experimental import pallas as pl
from jax.experimental.pallas import tpu as pltpu
from jax.sharding import PartitionSpec as P


ALPHA = 0.05
HIGHEST = lax.Precision.HIGHEST
STEPS = 32
BLOCKS = 32
TILE = 128
PACK = 40
VECS = 9
FIRST = 20
TURNED = [(i + FIRST) % BLOCKS for i in range(BLOCKS)]
ROWS2 = 2 * PACK
f32 = jnp.float32


def mm(x, y):
    return jnp.dot(x, y, precision=HIGHEST, preferred_element_type=f32)


def mm_nt(x, y):
    return lax.dot_general(x, y, (((1,), (1,)), ((), ())), precision=HIGHEST, preferred_element_type=f32)


def mm_tn(x, y):
    return lax.dot_general(x, y, (((0,), (0,)), ((), ())), precision=HIGHEST, preferred_element_type=f32)


def rows_of(shape):
    return lax.broadcasted_iota(jnp.int32, shape, 0)


def shift_down(x, by):
    return jnp.where(rows_of(x.shape) >= by, pltpu.roll(x, by, 0), 0.0)


def recurrence(x, decay):
    for by in (1, 2, 4, 8, 16):
        x = x + decay * shift_down(x, by)
        decay = decay * decay
    return x


def power_rows(decay, first, reverse=False):
    n = rows_of((STEPS, TILE))
    exponent = (STEPS - 1 - n if reverse else n) + first
    out = jnp.ones((STEPS, TILE), f32)
    for bit in range(6):
        out = out * jnp.where((exponent >> bit) & 1 == 1, decay, 1.0)
        decay = decay * decay
    return out


def to_32(decay):
    for _ in range(5):
        decay = decay * decay
    return decay


def picked(x, index_row):
    return jnp.take_along_axis(x, jnp.broadcast_to(index_row, x.shape), axis=1, mode="promise_in_bounds")


def params(coef, p):
    return coef[p : p + 1, :], coef[2 + p : 3 + p, :]


def coupled(p, low, high, own, side, links_ref, cond_ref, col):
    left = jnp.where(col == 1, side, 0.0) if p == 0 else own[0]
    right = own[1] if p == 0 else jnp.where(col == 0, side, 0.0)
    total = None
    for d, x in enumerate((low[p], high[p], left, right)):
        r = 2 * d + p
        term = cond_ref[r : r + 1, :] * picked(x, links_ref[r : r + 1, :])
        total = term if total is None else total + term
    return total


def every_other(ref, p, start=0):
    return ref[pl.ds(start + p, STEPS, stride=2), :]


def kernel_p(it, links, cond, init, values, cap, copies, own, links_out, cond_out, init_out, coef):
    own[...] = it[...]
    for k in range(4):
        copies[k * 2 * STEPS : (k + 1) * 2 * STEPS, :] = it[...]
    for p in range(2):
        capacity = jnp.broadcast_to(cap[0:1, p : p + 1], (1, TILE))
        gain = 1.0 / (values[p : p + 1, :] + capacity)
        coef[p : p + 1, :] = capacity * gain
        coef[2 + p : 3 + p, :] = gain
    links_out[...] = links[...]
    cond_out[...] = cond[...]
    init_out[...] = init[...]


def prepare(it, *rest):
    vmem = pl.BlockSpec(memory_space=pltpu.VMEM)
    return pl.pallas_call(
        kernel_p,
        out_shape=[
            jax.ShapeDtypeStruct((8 * STEPS, TILE), f32),
            pltpu.VMEM(it.shape, f32),
            *[pltpu.VMEM(x.shape, x.dtype) for x in rest[:3]],
            pltpu.VMEM((4, TILE), f32),
        ],
        in_specs=[vmem] * 6,
        out_specs=[vmem] * 6,
    )(it, *rest)


def quad_rows(start, count, height):
    odd, col = lax.axis_index("rows") % 2, lax.axis_index("cols")
    inner = ((1 - odd) * 2 + col) * 2 * height + start
    side = (odd * 2 + 1 - col) * 2 * height + jnp.where(col == 0, 0, height) + start
    return pl.ds(pl.multiple_of(inner, 8), count), pl.ds(pl.multiple_of(side, 8), count)


def kernel_a(it, src, quad, outer, bas, links, cond, init, coef, out, copies, near_basis):
    col = lax.axis_index("cols")
    block = lax.axis_index("tm")
    near_basis[...] = bas[pl.ds(pl.multiple_of((1 - col) * TILE, TILE), TILE), :]
    pair = lambda ref: [every_other(ref, p) for p in range(2)]
    chunk = lambda k: [every_other(quad, p, pl.multiple_of(k * 2 * STEPS, 2 * STEPS)) for p in range(2)]
    odd = lax.axis_index("rows") % 2
    inner, across, own = chunk((1 - odd) * 2 + col), chunk(odd * 2 + 1 - col), pair(it)
    sides = jnp.where(col == 0, across[0], across[1])
    lows, highs = zip(*(ordered(a, b) for a, b in zip(inner, pair(outer))))
    for p in range(2):
        basis = bas[p * TILE : (p + 1) * TILE, :]
        decay, gain = params(coef, p)
        force = every_other(src, p) + coupled(p, lows, highs, own, sides, links, cond, col)
        last = init[p : p + 1, :] - ALPHA * own[p][STEPS - 1 : STEPS, :]
        stacked = jnp.concatenate([force, jnp.broadcast_to(last, (8, TILE))], axis=0)
        modes = mm(stacked, basis)
        wrap = modes[STEPS : STEPS + 1, :]
        state = recurrence(modes[:STEPS] * gain, decay)
        end = state[STEPS - 1 : STEPS, :]
        end = jnp.where(block == BLOCKS - 1, ALPHA * end + wrap, end)
        row = rows_of((8, TILE))
        tail = jnp.where(row == 0, end, jnp.where(row == 1, decay, jnp.where(row == 2, wrap, 0.0)))
        first = mm_nt(state, basis)
        for ref, rows in ((out, ROWS2), (copies, 4 * ROWS2)):
            for at in range(p * PACK, rows, ROWS2):
                ref[at : at + STEPS, :] = first
                ref[at + STEPS : at + PACK, :] = tail


def kernel_b(src, own, quad, outer, bas, links, cond, coef, local, send):
    col = lax.axis_index("cols")
    block = lax.axis_index("tm")
    both = lambda ref, start, count: [ref[p * PACK + start : p * PACK + start + count, :] for p in range(2)]
    inner = lambda start, count: [quad[quad_rows(p * PACK + start, count, PACK)[0], :] for p in range(2)]
    side = lambda start, count: quad[quad_rows(start, count, PACK)[1], :]
    owns, sides = both(own, 0, STEPS), side(0, STEPS)
    lows, highs = zip(*(ordered(a, b) for a, b in zip(inner(0, STEPS), both(outer, 0, STEPS))))
    ends = (*both(own, STEPS, 8), *both(outer, STEPS, 8), *inner(STEPS, 8), side(STEPS, 8))
    vectors = [x[0:1, :] for x in ends]
    for p in range(2):
        basis = bas[p * TILE : (p + 1) * TILE, :]
        decay, gain = params(coef, p)
        force = every_other(src, p) + coupled(p, lows, highs, owns, sides, links, cond, col)
        state = recurrence(mm(force, basis) * gain, decay)
        local[p * STEPS : (p + 1) * STEPS, :] = state
        end = state[STEPS - 1 : STEPS, :]
        wrap = own[p * PACK + STEPS + 2 : p * PACK + STEPS + 3, :]
        vectors.append(jnp.where(block == BLOCKS - 1, ALPHA * end + wrap, end))
    for k, vector in enumerate(vectors):
        send[pl.ds(k, BLOCKS, stride=VECS), :] = jnp.broadcast_to(vector, (BLOCKS, TILE))


def matrices(p, neighbour, table, tie_rows, mask, bas, coef):
    basis = bas[p * TILE : (p + 1) * TILE, :]
    decay, gain = params(coef, p)
    link, weight = tie_rows
    weight = weight if mask is None else weight * mask
    direct = mm(weight * picked(neighbour.T, link), basis)
    return direct, direct * mm_tn(table, power_rows(decay, 0, reverse=True) * gain)


def ties_of(links, cond, low, high, odd):
    pick = lambda ref: jnp.where(odd, ref[high : high + 1, :], ref[low : low + 1, :])
    return pick(links), pick(cond)


def kernel_m(bas, outer, own2, quad, outer2, links, cond, coef, direct, through, tables, decays):
    odd = lax.axis_index("rows") % 2 == 1
    at = lambda x: x[1:2, :]
    both = lambda ref: [ref[p * PACK + STEPS : (p + 1) * PACK, :] for p in range(2)]
    inner = [quad[quad_rows(p * PACK + STEPS, 8, PACK)[0], :] for p in range(2)]
    side = quad[quad_rows(STEPS, 8, PACK)[1], :]
    for k, x in enumerate((*both(own2), *both(outer2), *inner, side)):
        decay = at(x)
        block_decay = to_32(decay)
        scale = 1.0 / (1.0 - ALPHA * to_32(block_decay))
        decays[k : k + 1, :] = block_decay
        tables[k * STEPS : (k + 1) * STEPS, :] = power_rows(decay, 1)
        tables[(7 + k) * STEPS : (8 + k) * STEPS, :] = power_rows(block_decay, 0) * scale
    decays[7:8, :] = jnp.zeros((1, TILE), f32)
    table = lambda k: tables[k * STEPS : (k + 1) * STEPS, :]
    for p in range(2):
        tile = lambda ref, q: ref[q * TILE : (q + 1) * TILE, :]
        near = 2 * (3 - p) + p
        for j, (neighbour, k, ties) in enumerate((
            (tile(outer, p), 2 + p, ties_of(links, cond, p, 2 + p, odd)),
            (tile(bas, 1 - p), 1 - p, ties_of(links, cond, near, near, odd)),
        )):
            rows = slice((2 * p + j) * TILE, (2 * p + j + 1) * TILE)
            direct[rows, :], through[rows, :] = matrices(p, neighbour, table(k), ties, None, bas, coef)


def kernel_n(bas, inner, side, tables, links, cond, coef, direct, through):
    odd = lax.axis_index("rows") % 2 == 1
    col = lax.axis_index("cols")
    table = lambda k: tables[k * STEPS : (k + 1) * STEPS, :]
    for p in range(2):
        far = 2 * (2 + p) + p
        outside = jnp.where(col == 1 - p, 1.0, 0.0)
        for j, (neighbour, k, ties, mask) in enumerate((
            (inner[p * TILE : (p + 1) * TILE, :], 4 + p, ties_of(links, cond, 2 + p, p, odd), None),
            (side[...], 6, ties_of(links, cond, far, far, odd), outside),
        )):
            rows = slice((2 * p + j) * TILE, (2 * p + j + 1) * TILE)
            direct[rows, :], through[rows, :] = matrices(p, neighbour, table(k), ties, mask, bas, coef)


def incoming(ends, block_decay, scaled_powers):
    summed = recurrence(ends, block_decay)
    start = ALPHA * block_decay * summed[BLOCKS - 2 : BLOCKS - 1, :] + ends[BLOCKS - 1 : BLOCKS, :]
    return shift_down(summed, 1) + scaled_powers * start


def row_at(x, index):
    return jnp.sum(jnp.where(rows_of(x.shape) == index, x, 0.0), axis=0, keepdims=True)


def kernel_c(received, local, direct1, through1, direct2, through2, tables, decays, bas, coef, out):
    block = lax.axis_index("tm")
    vector = lambda k: pltpu.roll(received[pl.ds(k, BLOCKS, stride=VECS), :], FIRST, 0)
    table = lambda k: tables[k * STEPS : (k + 1) * STEPS, :]
    states = [incoming(vector(k), decays[k : k + 1, :], table(7 + k)) for k in range(7)]
    paths = [table(k) * row_at(states[k], block) for k in range(7)]
    factor = jnp.where(rows_of((BLOCKS, TILE)) == BLOCKS - 1, ALPHA, 1.0)
    for p in range(2):
        basis = bas[p * TILE : (p + 1) * TILE, :]
        decay, gain = params(coef, p)
        span = slice(2 * p * TILE, 2 * (p + 1) * TILE)
        beside = lambda x, j, k: jnp.concatenate([x[j], x[k]], axis=1)
        product = lambda x, first, second: mm(beside(x, 2 + p, 1 - p), first[span, :]) + mm(
            beside(x, 4 + p, 6), second[span, :]
        )
        ends = vector(7 + p) + factor * product(states, through1, through2)
        entering = row_at(incoming(ends, decays[p : p + 1, :], table(7 + p)), block)
        force = product(paths, direct1, direct2)
        state = local[p * STEPS : (p + 1) * STEPS, :] + recurrence(force * gain, decay)
        state = state + table(p) * entering
        out[pl.ds(p, STEPS, stride=2), :] = mm_nt(state, basis)


def call(kernel, outs, *args, last=False):
    vmem = pl.BlockSpec(memory_space=pltpu.VMEM)
    shapes = [jax.ShapeDtypeStruct(out, f32) if last else pltpu.VMEM(out, f32) for out in outs]
    single = len(outs) == 1
    return pl.pallas_call(
        kernel,
        out_shape=shapes[0] if single else shapes,
        in_specs=[vmem] * len(args),
        out_specs=vmem if single else [vmem] * len(outs),
    )(*[pltpu.with_memory_space_constraint(arg, pltpu.VMEM) for arg in args])


def swaps(first):
    return [pair for i in range(first, lax.axis_size("rows") - 1, 2) for pair in ((i, i + 1), (i + 1, i))]


def ordered(inner, outer):
    odd = lax.axis_index("rows") % 2 == 1
    return jnp.where(odd, inner, outer), jnp.where(odd, outer, inner)


def on_device(iterate, source, initial, tile_basis, tile_values, capacity, tile_links, conductance):
    it = iterate.reshape(2 * STEPS, TILE)
    src = source.reshape(2 * STEPS, TILE)
    init = initial.reshape(2, TILE)
    bas = tile_basis.reshape(2 * TILE, TILE)
    values = tile_values.reshape(2, TILE)
    links = tile_links.reshape(8, TILE)
    cond = conductance.reshape(8, TILE)
    copies, own, links, cond, init, coef = prepare(it, links, cond, init, values, capacity)
    fours = [[4 * k + j for j in range(4)] for k in range(lax.axis_size("rows") // 2)]

    def exchange(own, copies):
        quad = lax.all_to_all(
            copies.reshape(4, *own.shape), ("rows", "cols"), split_axis=0, concat_axis=0, tiled=True,
            axis_index_groups=fours,
        )
        return quad.reshape(copies.shape), lax.ppermute(own, "rows", swaps(1))

    quad1, outer1 = exchange(own, copies)
    outer_basis = lax.ppermute(bas, "rows", swaps(1))
    own2, copies2, near_basis = call(
        kernel_a,
        [(ROWS2, TILE), (4 * ROWS2, TILE), (TILE, TILE)],
        own, src, quad1, outer1, bas, links, cond, init, coef,
    )
    quad, outer2 = exchange(own2, copies2)
    rows_basis, _ = lax.optimization_barrier((bas, own2))
    inner_basis = lax.ppermute(rows_basis, "rows", swaps(0))
    local, send = call(
        kernel_b,
        [(2 * STEPS, TILE), (BLOCKS * VECS, TILE)],
        src, own2, quad, outer2, bas, links, cond, coef,
    )
    flat = send.reshape(BLOCKS, VECS * TILE)
    received = lax.all_to_all(
        flat, "tm", split_axis=0, concat_axis=0, tiled=True, axis_index_groups=[TURNED]
    ).reshape(BLOCKS * VECS, TILE)
    near_basis, _ = lax.optimization_barrier((near_basis, send))
    side_basis = lax.ppermute(near_basis, "cols", [(0, 1), (1, 0)])
    pair_shape, table_shape = (4 * TILE, TILE), (14 * STEPS, TILE)
    direct1, through1, tables, decays = call(
        kernel_m,
        [pair_shape, pair_shape, table_shape, (8, TILE)],
        bas, outer_basis, own2, quad, outer2, links, cond, coef,
    )
    direct2, through2 = call(
        kernel_n, [pair_shape, pair_shape], bas, inner_basis, side_basis, tables, links, cond, coef
    )
    out = call(kernel_c, [(2 * STEPS, TILE)], received, local, direct1, through1, direct2, through2, tables, decays, bas, coef, last=True)
    return out.reshape(iterate.shape)


def solution(mesh):
    in_specs = (
        P("tm", "rows", "cols", None),
        P("tm", "rows", "cols", None),
        P("rows", "cols", None),
        P("rows", "cols", None, None),
        P("rows", "cols", None),
        P("rows", "cols"),
        P(None, "rows", "cols", None),
        P(None, "rows", "cols", None),
    )
    out_specs = P("tm", "rows", "cols", None)
    return jax.shard_map(on_device, mesh=mesh, in_specs=in_specs, out_specs=out_specs, check_vma=False)
```

```python
import jax
import jax.numpy as jnp
from jax import lax
from jax.experimental import pallas as pl
from jax.experimental.pallas import tpu as pltpu
from jax.sharding import PartitionSpec as P


ALPHA = 0.05
STEPS = 32
BLOCKS = 32
TILE = 128
PACK = 40
VECS = 9
FIRST = 20
TURNED = [(i + FIRST) % BLOCKS for i in range(BLOCKS)]
ROWS2 = 2 * PACK
f32 = jnp.float32


def halves(x):
    high = x.astype(jnp.bfloat16)
    return high, (x - high.astype(f32)).astype(jnp.bfloat16)


def product(x, y, left, right):
    (xh, xl), (yh, yl) = halves(x), halves(y)
    one = lambda p, q: lax.dot_general(p, q, (((left,), (right,)), ((), ())), preferred_element_type=f32)
    return one(xh, yh) + (one(xl, yh) + one(xh, yl))


def mm(x, y):
    return product(x, y, 1, 0)


def mm_nt(x, y):
    return product(x, y, 1, 1)


def mm_tn(x, y):
    return product(x, y, 0, 0)


def rows_of(shape):
    return lax.broadcasted_iota(jnp.int32, shape, 0)


def shift_down(x, by):
    return jnp.where(rows_of(x.shape) >= by, pltpu.roll(x, by, 0), 0.0)


def recurrence(x, decay):
    for by in (1, 2, 4, 8, 16):
        x = x + decay * shift_down(x, by)
        decay = decay * decay
    return x


def power_rows(decay, first, reverse=False):
    n = rows_of((STEPS, TILE))
    exponent = (STEPS - 1 - n if reverse else n) + first
    out = jnp.ones((STEPS, TILE), f32)
    for bit in range(6):
        out = out * jnp.where((exponent >> bit) & 1 == 1, decay, 1.0)
        decay = decay * decay
    return out


def to_32(decay):
    for _ in range(5):
        decay = decay * decay
    return decay


def picked(x, index_row):
    return jnp.take_along_axis(x, jnp.broadcast_to(index_row, x.shape), axis=1, mode="promise_in_bounds")


def params(coef, p):
    return coef[p : p + 1, :], coef[2 + p : 3 + p, :]


def coupled(p, low, high, own, side, links_ref, cond_ref, col):
    left = jnp.where(col == 1, side, 0.0) if p == 0 else own[0]
    right = own[1] if p == 0 else jnp.where(col == 0, side, 0.0)
    total = None
    for d, x in enumerate((low[p], high[p], left, right)):
        r = 2 * d + p
        term = cond_ref[r : r + 1, :] * picked(x, links_ref[r : r + 1, :])
        total = term if total is None else total + term
    return total


def every_other(ref, p, start=0):
    return ref[pl.ds(start + p, STEPS, stride=2), :]


def kernel_p(it, links, cond, init, values, cap, copies, own, links_out, cond_out, init_out, coef):
    own[...] = it[...]
    for k in range(4):
        copies[k * 2 * STEPS : (k + 1) * 2 * STEPS, :] = it[...]
    for p in range(2):
        capacity = jnp.broadcast_to(cap[0:1, p : p + 1], (1, TILE))
        gain = 1.0 / (values[p : p + 1, :] + capacity)
        coef[p : p + 1, :] = capacity * gain
        coef[2 + p : 3 + p, :] = gain
    links_out[...] = links[...]
    cond_out[...] = cond[...]
    init_out[...] = init[...]


def prepare(it, *rest):
    vmem = pl.BlockSpec(memory_space=pltpu.VMEM)
    return pl.pallas_call(
        kernel_p,
        out_shape=[
            jax.ShapeDtypeStruct((8 * STEPS, TILE), f32),
            pltpu.VMEM(it.shape, f32),
            *[pltpu.VMEM(x.shape, x.dtype) for x in rest[:3]],
            pltpu.VMEM((4, TILE), f32),
        ],
        in_specs=[vmem] * 6,
        out_specs=[vmem] * 6,
    )(it, *rest)


def quad_rows(start, count, height):
    odd, col = lax.axis_index("rows") % 2, lax.axis_index("cols")
    inner = ((1 - odd) * 2 + col) * 2 * height + start
    side = (odd * 2 + 1 - col) * 2 * height + jnp.where(col == 0, 0, height) + start
    return pl.ds(pl.multiple_of(inner, 8), count), pl.ds(pl.multiple_of(side, 8), count)


def kernel_a(it, src, quad, outer, bas, links, cond, init, coef, out, copies, near_basis):
    col = lax.axis_index("cols")
    block = lax.axis_index("tm")
    near_basis[...] = bas[pl.ds(pl.multiple_of((1 - col) * TILE, TILE), TILE), :]
    pair = lambda ref: [every_other(ref, p) for p in range(2)]
    chunk = lambda k: [every_other(quad, p, pl.multiple_of(k * 2 * STEPS, 2 * STEPS)) for p in range(2)]
    odd = lax.axis_index("rows") % 2
    inner, across, own = chunk((1 - odd) * 2 + col), chunk(odd * 2 + 1 - col), pair(it)
    sides = jnp.where(col == 0, across[0], across[1])
    lows, highs = zip(*(ordered(a, b) for a, b in zip(inner, pair(outer))))
    for p in range(2):
        basis = bas[p * TILE : (p + 1) * TILE, :]
        decay, gain = params(coef, p)
        force = every_other(src, p) + coupled(p, lows, highs, own, sides, links, cond, col)
        last = init[p : p + 1, :] - ALPHA * own[p][STEPS - 1 : STEPS, :]
        stacked = jnp.concatenate([force, jnp.broadcast_to(last, (8, TILE))], axis=0)
        modes = mm(stacked, basis)
        wrap = modes[STEPS : STEPS + 1, :]
        state = recurrence(modes[:STEPS] * gain, decay)
        end = state[STEPS - 1 : STEPS, :]
        end = jnp.where(block == BLOCKS - 1, ALPHA * end + wrap, end)
        row = rows_of((8, TILE))
        tail = jnp.where(row == 0, end, jnp.where(row == 1, decay, jnp.where(row == 2, wrap, 0.0)))
        first = mm_nt(state, basis)
        for ref, rows in ((out, ROWS2), (copies, 4 * ROWS2)):
            for at in range(p * PACK, rows, ROWS2):
                ref[at : at + STEPS, :] = first
                ref[at + STEPS : at + PACK, :] = tail


def kernel_b(src, own, quad, outer, bas, links, cond, coef, local, send):
    col = lax.axis_index("cols")
    block = lax.axis_index("tm")
    both = lambda ref, start, count: [ref[p * PACK + start : p * PACK + start + count, :] for p in range(2)]
    inner = lambda start, count: [quad[quad_rows(p * PACK + start, count, PACK)[0], :] for p in range(2)]
    side = lambda start, count: quad[quad_rows(start, count, PACK)[1], :]
    owns, sides = both(own, 0, STEPS), side(0, STEPS)
    lows, highs = zip(*(ordered(a, b) for a, b in zip(inner(0, STEPS), both(outer, 0, STEPS))))
    ends = (*both(own, STEPS, 8), *both(outer, STEPS, 8), *inner(STEPS, 8), side(STEPS, 8))
    vectors = [x[0:1, :] for x in ends]
    for p in range(2):
        basis = bas[p * TILE : (p + 1) * TILE, :]
        decay, gain = params(coef, p)
        force = every_other(src, p) + coupled(p, lows, highs, owns, sides, links, cond, col)
        state = recurrence(mm(force, basis) * gain, decay)
        local[p * STEPS : (p + 1) * STEPS, :] = state
        end = state[STEPS - 1 : STEPS, :]
        wrap = own[p * PACK + STEPS + 2 : p * PACK + STEPS + 3, :]
        vectors.append(jnp.where(block == BLOCKS - 1, ALPHA * end + wrap, end))
    for k, vector in enumerate(vectors):
        send[pl.ds(k, BLOCKS, stride=VECS), :] = jnp.broadcast_to(vector, (BLOCKS, TILE))


def matrices(p, neighbour, table, tie_rows, mask, bas, coef):
    basis = bas[p * TILE : (p + 1) * TILE, :]
    decay, gain = params(coef, p)
    link, weight = tie_rows
    weight = weight if mask is None else weight * mask
    direct = mm(weight * picked(neighbour.T, link), basis)
    return direct, direct * mm_tn(table, power_rows(decay, 0, reverse=True) * gain)


def ties_of(links, cond, low, high, odd):
    pick = lambda ref: jnp.where(odd, ref[high : high + 1, :], ref[low : low + 1, :])
    return pick(links), pick(cond)


def kernel_m(bas, outer, own2, quad, outer2, links, cond, coef, direct, through, tables, decays):
    odd = lax.axis_index("rows") % 2 == 1
    at = lambda x: x[1:2, :]
    both = lambda ref: [ref[p * PACK + STEPS : (p + 1) * PACK, :] for p in range(2)]
    inner = [quad[quad_rows(p * PACK + STEPS, 8, PACK)[0], :] for p in range(2)]
    side = quad[quad_rows(STEPS, 8, PACK)[1], :]
    for k, x in enumerate((*both(own2), *both(outer2), *inner, side)):
        decay = at(x)
        block_decay = to_32(decay)
        scale = 1.0 / (1.0 - ALPHA * to_32(block_decay))
        decays[k : k + 1, :] = block_decay
        tables[k * STEPS : (k + 1) * STEPS, :] = power_rows(decay, 1)
        tables[(7 + k) * STEPS : (8 + k) * STEPS, :] = power_rows(block_decay, 0) * scale
    decays[7:8, :] = jnp.zeros((1, TILE), f32)
    table = lambda k: tables[k * STEPS : (k + 1) * STEPS, :]
    for p in range(2):
        tile = lambda ref, q: ref[q * TILE : (q + 1) * TILE, :]
        near = 2 * (3 - p) + p
        for j, (neighbour, k, ties) in enumerate((
            (tile(outer, p), 2 + p, ties_of(links, cond, p, 2 + p, odd)),
            (tile(bas, 1 - p), 1 - p, ties_of(links, cond, near, near, odd)),
        )):
            rows = slice((2 * p + j) * TILE, (2 * p + j + 1) * TILE)
            direct[rows, :], through[rows, :] = matrices(p, neighbour, table(k), ties, None, bas, coef)


def kernel_n(bas, inner, side, tables, links, cond, coef, direct, through):
    odd = lax.axis_index("rows") % 2 == 1
    col = lax.axis_index("cols")
    table = lambda k: tables[k * STEPS : (k + 1) * STEPS, :]
    for p in range(2):
        far = 2 * (2 + p) + p
        outside = jnp.where(col == 1 - p, 1.0, 0.0)
        for j, (neighbour, k, ties, mask) in enumerate((
            (inner[p * TILE : (p + 1) * TILE, :], 4 + p, ties_of(links, cond, 2 + p, p, odd), None),
            (side[...], 6, ties_of(links, cond, far, far, odd), outside),
        )):
            rows = slice((2 * p + j) * TILE, (2 * p + j + 1) * TILE)
            direct[rows, :], through[rows, :] = matrices(p, neighbour, table(k), ties, mask, bas, coef)


def incoming(ends, block_decay, scaled_powers):
    summed = recurrence(ends, block_decay)
    start = ALPHA * block_decay * summed[BLOCKS - 2 : BLOCKS - 1, :] + ends[BLOCKS - 1 : BLOCKS, :]
    return shift_down(summed, 1) + scaled_powers * start


def row_at(x, index):
    return jnp.sum(jnp.where(rows_of(x.shape) == index, x, 0.0), axis=0, keepdims=True)


def kernel_c(received, local, direct1, through1, direct2, through2, tables, decays, bas, coef, out):
    block = lax.axis_index("tm")
    vector = lambda k: pltpu.roll(received[pl.ds(k, BLOCKS, stride=VECS), :], FIRST, 0)
    table = lambda k: tables[k * STEPS : (k + 1) * STEPS, :]
    states = [incoming(vector(k), decays[k : k + 1, :], table(7 + k)) for k in range(7)]
    paths = [table(k) * row_at(states[k], block) for k in range(7)]
    factor = jnp.where(rows_of((BLOCKS, TILE)) == BLOCKS - 1, ALPHA, 1.0)
    for p in range(2):
        basis = bas[p * TILE : (p + 1) * TILE, :]
        decay, gain = params(coef, p)
        span = slice(2 * p * TILE, 2 * (p + 1) * TILE)
        beside = lambda x, j, k: jnp.concatenate([x[j], x[k]], axis=1)
        joined = lambda x, first, second: mm(beside(x, 2 + p, 1 - p), first[span, :]) + mm(
            beside(x, 4 + p, 6), second[span, :]
        )
        ends = vector(7 + p) + factor * joined(states, through1, through2)
        entering = row_at(incoming(ends, decays[p : p + 1, :], table(7 + p)), block)
        force = joined(paths, direct1, direct2)
        state = local[p * STEPS : (p + 1) * STEPS, :] + recurrence(force * gain, decay)
        state = state + table(p) * entering
        out[pl.ds(p, STEPS, stride=2), :] = mm_nt(state, basis)


def call(kernel, outs, *args, last=False):
    vmem = pl.BlockSpec(memory_space=pltpu.VMEM)
    shapes = [jax.ShapeDtypeStruct(out, f32) if last else pltpu.VMEM(out, f32) for out in outs]
    single = len(outs) == 1
    return pl.pallas_call(
        kernel,
        out_shape=shapes[0] if single else shapes,
        in_specs=[vmem] * len(args),
        out_specs=vmem if single else [vmem] * len(outs),
    )(*[pltpu.with_memory_space_constraint(arg, pltpu.VMEM) for arg in args])


def swaps(first):
    return [pair for i in range(first, lax.axis_size("rows") - 1, 2) for pair in ((i, i + 1), (i + 1, i))]


def ordered(inner, outer):
    odd = lax.axis_index("rows") % 2 == 1
    return jnp.where(odd, inner, outer), jnp.where(odd, outer, inner)


def on_device(iterate, source, initial, tile_basis, tile_values, capacity, tile_links, conductance):
    it = iterate.reshape(2 * STEPS, TILE)
    src = source.reshape(2 * STEPS, TILE)
    init = initial.reshape(2, TILE)
    bas = tile_basis.reshape(2 * TILE, TILE)
    values = tile_values.reshape(2, TILE)
    links = tile_links.reshape(8, TILE)
    cond = conductance.reshape(8, TILE)
    copies, own, links, cond, init, coef = prepare(it, links, cond, init, values, capacity)
    fours = [[4 * k + j for j in range(4)] for k in range(lax.axis_size("rows") // 2)]

    def exchange(own, copies):
        quad = lax.all_to_all(
            copies.reshape(4, *own.shape), ("rows", "cols"), split_axis=0, concat_axis=0, tiled=True,
            axis_index_groups=fours,
        )
        return quad.reshape(copies.shape), lax.ppermute(own, "rows", swaps(1))

    quad1, outer1 = exchange(own, copies)
    outer_basis = lax.ppermute(bas, "rows", swaps(1))
    own2, copies2, near_basis = call(
        kernel_a,
        [(ROWS2, TILE), (4 * ROWS2, TILE), (TILE, TILE)],
        own, src, quad1, outer1, bas, links, cond, init, coef,
    )
    quad, outer2 = exchange(own2, copies2)
    rows_basis, _ = lax.optimization_barrier((bas, own2))
    inner_basis = lax.ppermute(rows_basis, "rows", swaps(0))
    local, send = call(
        kernel_b,
        [(2 * STEPS, TILE), (BLOCKS * VECS, TILE)],
        src, own2, quad, outer2, bas, links, cond, coef,
    )
    flat = send.reshape(BLOCKS, VECS * TILE)
    received = lax.all_to_all(
        flat, "tm", split_axis=0, concat_axis=0, tiled=True, axis_index_groups=[TURNED]
    ).reshape(BLOCKS * VECS, TILE)
    near_basis, _ = lax.optimization_barrier((near_basis, send))
    side_basis = lax.ppermute(near_basis, "cols", [(0, 1), (1, 0)])
    pair_shape, table_shape = (4 * TILE, TILE), (14 * STEPS, TILE)
    direct1, through1, tables, decays = call(
        kernel_m,
        [pair_shape, pair_shape, table_shape, (8, TILE)],
        bas, outer_basis, own2, quad, outer2, links, cond, coef,
    )
    direct2, through2 = call(
        kernel_n, [pair_shape, pair_shape], bas, inner_basis, side_basis, tables, links, cond, coef
    )
    out = call(kernel_c, [(2 * STEPS, TILE)], received, local, direct1, through1, direct2, through2, tables, decays, bas, coef, last=True)
    return out.reshape(iterate.shape)


def solution(mesh):
    in_specs = (
        P("tm", "rows", "cols", None),
        P("tm", "rows", "cols", None),
        P("rows", "cols", None),
        P("rows", "cols", None, None),
        P("rows", "cols", None),
        P("rows", "cols"),
        P(None, "rows", "cols", None),
        P(None, "rows", "cols", None),
    )
    out_specs = P("tm", "rows", "cols", None)
    return jax.shard_map(on_device, mesh=mesh, in_specs=in_specs, out_specs=out_specs, check_vma=False)
```

```python
import jax
import jax.numpy as jnp
from jax import lax
from jax.experimental import pallas as pl
from jax.experimental.pallas import tpu as pltpu
from jax.sharding import PartitionSpec as P


ALPHA = 0.05
STEPS = 32
BLOCKS = 32
TILE = 128
PACK = 40
VECS = 9
FIRST = 20
TURNED = [(i + FIRST) % BLOCKS for i in range(BLOCKS)]
ROWS2 = 2 * PACK
f32 = jnp.float32


def halves(x):
    high = x.astype(jnp.bfloat16)
    return high, (x - high.astype(f32)).astype(jnp.bfloat16)


def product(x, y, left, right):
    (xh, xl), (yh, yl) = halves(x), y if isinstance(y, tuple) else halves(y)
    one = lambda p, q: lax.dot_general(p, q, (((left,), (right,)), ((), ())), preferred_element_type=f32)
    return one(xh, yh) + (one(xl, yh) + one(xh, yl))


def mm(x, y):
    return product(x, y, 1, 0)


def mm_nt(x, y):
    return product(x, y, 1, 1)


def mm_tn(x, y):
    return product(x, y, 0, 0)


def rows_of(shape):
    return lax.broadcasted_iota(jnp.int32, shape, 0)


def shift_down(x, by):
    return jnp.where(rows_of(x.shape) >= by, pltpu.roll(x, by, 0), 0.0)


def recurrence(x, decay):
    for by in (1, 2, 4, 8, 16):
        x = x + decay * shift_down(x, by)
        decay = decay * decay
    return x


def power_rows(decay, first, reverse=False):
    n = rows_of((STEPS, TILE))
    exponent = (STEPS - 1 - n if reverse else n) + first
    out = jnp.ones((STEPS, TILE), f32)
    for bit in range(6):
        out = out * jnp.where((exponent >> bit) & 1 == 1, decay, 1.0)
        decay = decay * decay
    return out


def to_32(decay):
    for _ in range(5):
        decay = decay * decay
    return decay


def picked(x, index_row):
    return jnp.take_along_axis(x, jnp.broadcast_to(index_row, x.shape), axis=1, mode="promise_in_bounds")


def params(coef, p):
    return coef[p : p + 1, :], coef[2 + p : 3 + p, :]


def coupled(p, low, high, own, side, links_ref, cond_ref, col):
    left = jnp.where(col == 1, side, 0.0) if p == 0 else own[0]
    right = own[1] if p == 0 else jnp.where(col == 0, side, 0.0)
    total = None
    for d, x in enumerate((low[p], high[p], left, right)):
        r = 2 * d + p
        term = cond_ref[r : r + 1, :] * picked(x, links_ref[r : r + 1, :])
        total = term if total is None else total + term
    return total


def every_other(ref, p, start=0):
    return ref[pl.ds(start + p, STEPS, stride=2), :]


def kernel_p(it, links, cond, init, values, cap, copies, own, links_out, cond_out, init_out, coef):
    own[...] = it[...]
    for k in range(4):
        copies[k * 2 * STEPS : (k + 1) * 2 * STEPS, :] = it[...]
    for p in range(2):
        capacity = jnp.broadcast_to(cap[0:1, p : p + 1], (1, TILE))
        gain = 1.0 / (values[p : p + 1, :] + capacity)
        coef[p : p + 1, :] = capacity * gain
        coef[2 + p : 3 + p, :] = gain
    links_out[...] = links[...]
    cond_out[...] = cond[...]
    init_out[...] = init[...]


def prepare(it, *rest):
    vmem = pl.BlockSpec(memory_space=pltpu.VMEM)
    return pl.pallas_call(
        kernel_p,
        out_shape=[
            jax.ShapeDtypeStruct((8 * STEPS, TILE), f32),
            pltpu.VMEM(it.shape, f32),
            *[pltpu.VMEM(x.shape, x.dtype) for x in rest[:3]],
            pltpu.VMEM((4, TILE), f32),
        ],
        in_specs=[vmem] * 6,
        out_specs=[vmem] * 6,
    )(it, *rest)


def quad_rows(start, count, height):
    odd, col = lax.axis_index("rows") % 2, lax.axis_index("cols")
    inner = ((1 - odd) * 2 + col) * 2 * height + start
    side = (odd * 2 + 1 - col) * 2 * height + jnp.where(col == 0, 0, height) + start
    return pl.ds(pl.multiple_of(inner, 8), count), pl.ds(pl.multiple_of(side, 8), count)


def kernel_a(it, src, quad, outer, bas, links, cond, init, coef, out, copies, near_basis):
    col = lax.axis_index("cols")
    block = lax.axis_index("tm")
    near_basis[...] = bas[pl.ds(pl.multiple_of((1 - col) * TILE, TILE), TILE), :]
    pair = lambda ref: [every_other(ref, p) for p in range(2)]
    chunk = lambda k: [every_other(quad, p, pl.multiple_of(k * 2 * STEPS, 2 * STEPS)) for p in range(2)]
    odd = lax.axis_index("rows") % 2
    inner, across, own = chunk((1 - odd) * 2 + col), chunk(odd * 2 + 1 - col), pair(it)
    sides = jnp.where(col == 0, across[0], across[1])
    lows, highs = zip(*(ordered(a, b) for a, b in zip(inner, pair(outer))))
    for p in range(2):
        basis = bas[p * TILE : (p + 1) * TILE, :]
        decay, gain = params(coef, p)
        force = every_other(src, p) + coupled(p, lows, highs, own, sides, links, cond, col)
        last = init[p : p + 1, :] - ALPHA * own[p][STEPS - 1 : STEPS, :]
        stacked = jnp.concatenate([force, jnp.broadcast_to(last, (8, TILE))], axis=0)
        modes = mm(stacked, basis)
        wrap = modes[STEPS : STEPS + 1, :]
        state = recurrence(modes[:STEPS] * gain, decay)
        end = state[STEPS - 1 : STEPS, :]
        end = jnp.where(block == BLOCKS - 1, ALPHA * end + wrap, end)
        row = rows_of((8, TILE))
        tail = jnp.where(row == 0, end, jnp.where(row == 1, decay, jnp.where(row == 2, wrap, 0.0)))
        first = mm_nt(state, basis)
        for ref, rows in ((out, ROWS2), (copies, 4 * ROWS2)):
            for at in range(p * PACK, rows, ROWS2):
                ref[at : at + STEPS, :] = first
                ref[at + STEPS : at + PACK, :] = tail


def kernel_b(src, own, quad, outer, bas, links, cond, coef, local, send):
    col = lax.axis_index("cols")
    block = lax.axis_index("tm")
    both = lambda ref, start, count: [ref[p * PACK + start : p * PACK + start + count, :] for p in range(2)]
    inner = lambda start, count: [quad[quad_rows(p * PACK + start, count, PACK)[0], :] for p in range(2)]
    side = lambda start, count: quad[quad_rows(start, count, PACK)[1], :]
    owns, sides = both(own, 0, STEPS), side(0, STEPS)
    lows, highs = zip(*(ordered(a, b) for a, b in zip(inner(0, STEPS), both(outer, 0, STEPS))))
    ends = (*both(own, STEPS, 8), *both(outer, STEPS, 8), *inner(STEPS, 8), side(STEPS, 8))
    vectors = [x[0:1, :] for x in ends]
    for p in range(2):
        basis = bas[p * TILE : (p + 1) * TILE, :]
        decay, gain = params(coef, p)
        force = every_other(src, p) + coupled(p, lows, highs, owns, sides, links, cond, col)
        state = recurrence(mm(force, basis) * gain, decay)
        local[p * STEPS : (p + 1) * STEPS, :] = state
        end = state[STEPS - 1 : STEPS, :]
        wrap = own[p * PACK + STEPS + 2 : p * PACK + STEPS + 3, :]
        vectors.append(jnp.where(block == BLOCKS - 1, ALPHA * end + wrap, end))
    for k, vector in enumerate(vectors):
        send[pl.ds(k, BLOCKS, stride=VECS), :] = jnp.broadcast_to(vector, (BLOCKS, TILE))


def matrices(p, neighbour, table, tie_rows, mask, bas, coef):
    basis = bas[p * TILE : (p + 1) * TILE, :]
    decay, gain = params(coef, p)
    link, weight = tie_rows
    weight = weight if mask is None else weight * mask
    direct = mm(weight * picked(neighbour.T, link), basis)
    return direct, direct * mm_tn(table, power_rows(decay, 0, reverse=True) * gain)


def ties_of(links, cond, low, high, odd):
    pick = lambda ref: jnp.where(odd, ref[high : high + 1, :], ref[low : low + 1, :])
    return pick(links), pick(cond)


def store(ref, rows, high, low):
    ref[rows, :] = high
    at = ref.shape[0] // 2
    ref[rows.start + at : rows.stop + at, :] = low


def load(ref, rows):
    at = ref.shape[0] // 2
    return ref[rows, :], ref[rows.start + at : rows.stop + at, :]


def kernel_m(bas, outer, own2, quad, outer2, links, cond, coef, direct, through, turned, tables, decays):
    odd = lax.axis_index("rows") % 2 == 1
    at = lambda x: x[1:2, :]
    both = lambda ref: [ref[p * PACK + STEPS : (p + 1) * PACK, :] for p in range(2)]
    inner = [quad[quad_rows(p * PACK + STEPS, 8, PACK)[0], :] for p in range(2)]
    side = quad[quad_rows(STEPS, 8, PACK)[1], :]
    for k, x in enumerate((*both(own2), *both(outer2), *inner, side)):
        decay = at(x)
        block_decay = to_32(decay)
        scale = 1.0 / (1.0 - ALPHA * to_32(block_decay))
        decays[k : k + 1, :] = block_decay
        tables[k * STEPS : (k + 1) * STEPS, :] = power_rows(decay, 1)
        tables[(7 + k) * STEPS : (8 + k) * STEPS, :] = power_rows(block_decay, 0) * scale
    decays[7:8, :] = jnp.zeros((1, TILE), f32)
    table = lambda k: tables[k * STEPS : (k + 1) * STEPS, :]
    for p in range(2):
        store(turned, slice(p * TILE, (p + 1) * TILE), *halves(bas[p * TILE : (p + 1) * TILE, :].T))
        tile = lambda ref, q: ref[q * TILE : (q + 1) * TILE, :]
        near = 2 * (3 - p) + p
        for j, (neighbour, k, ties) in enumerate((
            (tile(outer, p), 2 + p, ties_of(links, cond, p, 2 + p, odd)),
            (tile(bas, 1 - p), 1 - p, ties_of(links, cond, near, near, odd)),
        )):
            made = matrices(p, neighbour, table(k), ties, None, bas, coef)
            rows = slice((2 * p + j) * TILE, (2 * p + j + 1) * TILE)
            store(direct, rows, *halves(made[0]))
            store(through, rows, *halves(made[1]))


def kernel_n(bas, inner, side, tables, links, cond, coef, direct, through):
    odd = lax.axis_index("rows") % 2 == 1
    col = lax.axis_index("cols")
    table = lambda k: tables[k * STEPS : (k + 1) * STEPS, :]
    for p in range(2):
        far = 2 * (2 + p) + p
        outside = jnp.where(col == 1 - p, 1.0, 0.0)
        for j, (neighbour, k, ties, mask) in enumerate((
            (inner[p * TILE : (p + 1) * TILE, :], 4 + p, ties_of(links, cond, 2 + p, p, odd), None),
            (side[...], 6, ties_of(links, cond, far, far, odd), outside),
        )):
            made = matrices(p, neighbour, table(k), ties, mask, bas, coef)
            rows = slice((2 * p + j) * TILE, (2 * p + j + 1) * TILE)
            store(direct, rows, *halves(made[0]))
            store(through, rows, *halves(made[1]))


def incoming(ends, block_decay, scaled_powers):
    summed = recurrence(ends, block_decay)
    start = ALPHA * block_decay * summed[BLOCKS - 2 : BLOCKS - 1, :] + ends[BLOCKS - 1 : BLOCKS, :]
    return shift_down(summed, 1) + scaled_powers * start


def row_at(x, index):
    return jnp.sum(jnp.where(rows_of(x.shape) == index, x, 0.0), axis=0, keepdims=True)


def kernel_c(received, local, direct1, through1, direct2, through2, turned, tables, decays, coef, out):
    block = lax.axis_index("tm")
    vector = lambda k: pltpu.roll(received[pl.ds(k, BLOCKS, stride=VECS), :], FIRST, 0)
    table = lambda k: tables[k * STEPS : (k + 1) * STEPS, :]
    states = [incoming(vector(k), decays[k : k + 1, :], table(7 + k)) for k in range(7)]
    paths = [table(k) * row_at(states[k], block) for k in range(7)]
    factor = jnp.where(rows_of((BLOCKS, TILE)) == BLOCKS - 1, ALPHA, 1.0)
    for p in range(2):
        decay, gain = params(coef, p)
        span = slice(2 * p * TILE, 2 * (p + 1) * TILE)
        beside = lambda x, j, k: jnp.concatenate([x[j], x[k]], axis=1)
        joined = lambda x, first, second: mm(beside(x, 2 + p, 1 - p), load(first, span)) + mm(
            beside(x, 4 + p, 6), load(second, span)
        )
        ends = vector(7 + p) + factor * joined(states, through1, through2)
        entering = row_at(incoming(ends, decays[p : p + 1, :], table(7 + p)), block)
        force = joined(paths, direct1, direct2)
        state = local[p * STEPS : (p + 1) * STEPS, :] + recurrence(force * gain, decay)
        state = state + table(p) * entering
        out[pl.ds(p, STEPS, stride=2), :] = mm(state, load(turned, slice(p * TILE, (p + 1) * TILE)))


def call(kernel, outs, *args, last=False):
    vmem = pl.BlockSpec(memory_space=pltpu.VMEM)
    shapes = [jax.ShapeDtypeStruct(out[:2], f32) if last else pltpu.VMEM(out[:2], *(out[2:] or (f32,))) for out in outs]
    single = len(outs) == 1
    return pl.pallas_call(
        kernel,
        out_shape=shapes[0] if single else shapes,
        in_specs=[vmem] * len(args),
        out_specs=vmem if single else [vmem] * len(outs),
    )(*[pltpu.with_memory_space_constraint(arg, pltpu.VMEM) for arg in args])


def swaps(first):
    return [pair for i in range(first, lax.axis_size("rows") - 1, 2) for pair in ((i, i + 1), (i + 1, i))]


def ordered(inner, outer):
    odd = lax.axis_index("rows") % 2 == 1
    return jnp.where(odd, inner, outer), jnp.where(odd, outer, inner)


def on_device(iterate, source, initial, tile_basis, tile_values, capacity, tile_links, conductance):
    it = iterate.reshape(2 * STEPS, TILE)
    src = source.reshape(2 * STEPS, TILE)
    init = initial.reshape(2, TILE)
    bas = tile_basis.reshape(2 * TILE, TILE)
    values = tile_values.reshape(2, TILE)
    links = tile_links.reshape(8, TILE)
    cond = conductance.reshape(8, TILE)
    copies, own, links, cond, init, coef = prepare(it, links, cond, init, values, capacity)
    fours = [[4 * k + j for j in range(4)] for k in range(lax.axis_size("rows") // 2)]

    def exchange(own, copies):
        quad = lax.all_to_all(
            copies.reshape(4, *own.shape), ("rows", "cols"), split_axis=0, concat_axis=0, tiled=True,
            axis_index_groups=fours,
        )
        return quad.reshape(copies.shape), lax.ppermute(own, "rows", swaps(1))

    quad1, outer1 = exchange(own, copies)
    outer_basis = lax.ppermute(bas, "rows", swaps(1))
    own2, copies2, near_basis = call(
        kernel_a,
        [(ROWS2, TILE), (4 * ROWS2, TILE), (TILE, TILE)],
        own, src, quad1, outer1, bas, links, cond, init, coef,
    )
    quad, outer2 = exchange(own2, copies2)
    rows_basis, _ = lax.optimization_barrier((bas, own2))
    inner_basis = lax.ppermute(rows_basis, "rows", swaps(0))
    local, send = call(
        kernel_b,
        [(2 * STEPS, TILE), (BLOCKS * VECS, TILE)],
        src, own2, quad, outer2, bas, links, cond, coef,
    )
    flat = send.reshape(BLOCKS, VECS * TILE)
    received = lax.all_to_all(
        flat, "tm", split_axis=0, concat_axis=0, tiled=True, axis_index_groups=[TURNED]
    ).reshape(BLOCKS * VECS, TILE)
    near_basis, _ = lax.optimization_barrier((near_basis, send))
    side_basis = lax.ppermute(near_basis, "cols", [(0, 1), (1, 0)])
    pair_shape, table_shape = (8 * TILE, TILE, jnp.bfloat16), (14 * STEPS, TILE)
    direct1, through1, turned, tables, decays = call(
        kernel_m,
        [pair_shape, pair_shape, (4 * TILE, TILE, jnp.bfloat16), table_shape, (8, TILE)],
        bas, outer_basis, own2, quad, outer2, links, cond, coef,
    )
    direct2, through2 = call(
        kernel_n, [pair_shape, pair_shape], bas, inner_basis, side_basis, tables, links, cond, coef
    )
    out = call(kernel_c, [(2 * STEPS, TILE)], received, local, direct1, through1, direct2, through2, turned, tables, decays, coef, last=True)
    return out.reshape(iterate.shape)


def solution(mesh):
    in_specs = (
        P("tm", "rows", "cols", None),
        P("tm", "rows", "cols", None),
        P("rows", "cols", None),
        P("rows", "cols", None, None),
        P("rows", "cols", None),
        P("rows", "cols"),
        P(None, "rows", "cols", None),
        P(None, "rows", "cols", None),
    )
    out_specs = P("tm", "rows", "cols", None)
    return jax.shard_map(on_device, mesh=mesh, in_specs=in_specs, out_specs=out_specs, check_vma=False)
```
